128 devices in a mesh: expert: 8 (over z, core), hidden: 16 (over x, y).
Axes of the slice: x: 4, y: 4, z: 4, core: 2. Of those that a mesh axis runs over, the one named last changes fastest.
Arguments:
- queries: bfloat16 [512, 4096], P('expert', 'hidden'), may hold values from -1000 to 1000
- new_key: bfloat16 [512, 4096], P('expert', 'hidden'), may hold values from -12 to 12
- new_value: bfloat16 [512, 4096], P('expert', 'hidden'), may hold values from -6 to 6
- key_cache: bfloat16 [512, 32, 64, 128], P('expert', 'hidden'), may hold values from -12 to 12
- value_cache: bfloat16 [512, 32, 64, 128], P('expert', 'hidden'), may hold values from -6 to 6
- cache_lengths: int32 [512], P('expert'), may hold values from 1 to 64, as said below
- residual: bfloat16 [512, 4096], P('expert'), may hold values from -1.5 to 1.5
- out_weight: bfloat16 [4096, 4096], P('hidden'), may hold values from -0.125 to 0.125
- norm_gain: bfloat16 [4096], replicated, may hold values from 0.25 to 1.75
- expert_ids: int32 [512, 2], P('expert'), may hold values from 0 to 7, all different within a row; in each aligned block of 64 rows (0 to 63, 64 to 127, ...) at most 32 rows name the same one
- gate_weight: bfloat16 [8, 4096, 11008], P('expert', None, 'hidden'), may hold values from -0.09375 to 0.09375
- up_weight: bfloat16 [8, 4096, 11008], P('expert', None, 'hidden'), may hold values from -0.09375 to 0.09375
- down_weight: bfloat16 [8, 11008, 4096], P('expert', 'hidden'), may hold values from -0.078125 to 0.078125
Outputs:
- layer_out: bfloat16 [512, 4096], P('expert', 'hidden')
The draws below stay inside these ranges and needn't reach their ends.
Inputs may be any that keep to these rules, and one draw needn't show every extreme that they name: `expert_ids`: each row names two different experts; within each aligned block of 64 rows no expert is named by more than 32 rows, and in every draw some expert is named by exactly 32 rows of some block. Request r attends its cached positions 0 to cache_lengths[r] - 1 and its own new key; some request has exactly 64.
All inputs are finite; a program needn't handle non-finite values.
Results may differ from the reference program's by a relative error of at most 0.012.
Values may be sent and summed in bfloat16 or wider, within the bound.
No kernel may reach another device: no remote copies, remote signals or barrier semaphores. Data moves between devices by JAX's collectives and lax.ppermute only.
A program may use at most 128 MiB of HBM per device.

```python
import math
import jax
import jax.numpy as jnp
import numpy as np
from jax import lax

D = 4096
FF = 11008
HEADS = 32
HD = 128
REQ_DEV = 64
CACHE_LEN = 64
EXPERTS = 8
ROWS = 512
CAP = 32
N_EXPERT = 8


def draw_queries(key, part):
    values = jax.random.normal(jax.random.fold_in(key, 101), (ROWS, HEADS, HD), jnp.float32)
    return values.reshape(ROWS, HEADS * HD).astype(jnp.bfloat16)


def draw_new_key(key, part):
    values = jax.random.normal(jax.random.fold_in(key, 102), (ROWS, HEADS, HD), jnp.float32)
    return jnp.clip(values, -12.0, 12.0).reshape(ROWS, HEADS * HD).astype(jnp.bfloat16)


def draw_key_cache(key, part):
    values = jax.random.normal(jax.random.fold_in(key, 103), (ROWS, HEADS, CACHE_LEN, HD), jnp.float32)
    return jnp.clip(values, -12.0, 12.0).astype(jnp.bfloat16)


def draw_cache_lengths(key, part):
    key_limit, key_length, key_choose = jax.random.split(jax.random.fold_in(key, 104), 3)
    limits = jax.random.randint(key_limit, (ROWS // REQ_DEV, 1), CACHE_LEN // 4, CACHE_LEN + 1)
    limits = jnp.broadcast_to(limits, (ROWS // REQ_DEV, REQ_DEV)).reshape(ROWS)
    drawn = jax.random.randint(key_length, (ROWS,), 0, 1 << 20)
    lengths = 1 + drawn % limits
    longest = jax.random.randint(key_choose, (), 0, ROWS)
    return jnp.where(jnp.arange(ROWS) == longest, CACHE_LEN, lengths).astype(jnp.int32)


def spiked(result, stream_key, source, target, blocks, factor):
    def block_of(dim):
        return (jnp.arange(result.shape[dim]) // (result.shape[dim] // blocks)).reshape((-1,) + (1,) * (result.ndim - 1 - dim))

    one_side = jax.random.permutation(stream_key, blocks)[block_of(target)]
    second = (block_of(target) + blocks // 2) % blocks
    return jnp.where((block_of(source) == one_side) | (block_of(source) == second), factor * result, result)


def level_of(key, extent, cuts, least, high):
    def one(axis_at, blocks):
        steps = jax.random.uniform(jax.random.fold_in(jax.random.fold_in(key, 6), axis_at), (blocks,), jnp.float32, least / len(cuts), high / len(cuts))
        return jnp.repeat(jnp.exp(steps), extent[axis_at] // blocks).reshape((-1,) + (1,) * (len(extent) - axis_at - 1))

    gain = one(*cuts[0])
    for cut in cuts[1:]:
        gain = gain * one(*cut)
    return gain


def routed_block(key, own, number, rows, number_of, top, bound, skew):
    sequence = jax.random.permutation(key, number_of)
    crowded, common = shares(number_of, rows * top, bound, skew, True), shares(number_of, rows * top, bound, skew, False)
    places = jnp.arange(number_of)

    def named(sizes, rotation):
        used = int((sizes > 0).sum())
        fixed = max(1, used // 4)
        passed = fixed + (places - fixed + rotation * (used - fixed)) % max(1, number_of - fixed)
        return jnp.zeros((number_of,), jnp.int32).at[sequence[jnp.where(places < fixed, places, passed)]].set(jnp.asarray(sizes, jnp.int32))

    sizes = jnp.where(number % 4 == 0, named(crowded, number // 4), named(common, number - number // 4 - 1))
    mixed = jax.random.permutation(jax.random.fold_in(own, 3), number_of)
    giver, taker = mixed[0:number_of // 2 * 2:2], mixed[1:number_of // 2 * 2:2]
    room = jnp.minimum(sizes[giver] - 1, bound - sizes[taker]) // 2
    room = jnp.where((giver == sequence[0]) | (taker == sequence[0]) | (sizes[taker] == 0), 0, jnp.maximum(room, 0))
    passed = jax.random.randint(jax.random.fold_in(own, 4), (number_of // 2,), 0, 1 << 20) % (room + 1)
    sizes = sizes.at[giver].add(-passed).at[taker].add(passed)
    items = jnp.searchsorted(jnp.cumsum(sizes), jnp.arange(rows * top), side="right").astype(jnp.int32)
    table = items.reshape(top, rows).T
    table = table[jax.random.permutation(jax.random.fold_in(own, 1), rows)]
    rotation = jax.random.randint(jax.random.fold_in(own, 2), (rows, 1), 0, top)
    return jnp.take_along_axis(table, (jnp.arange(top)[None, :] + rotation) % top, axis=1)


def shares(amount, total, reach, lean, full):
    portions = [(1 << 20) // math.isqrt(rank ** lean) + 1 for rank in range(1, amount + 1)]
    largest = reach if full else min(reach, max(-(-total // amount), total * portions[0] // sum(portions)))
    least = 1 if total - largest >= amount - 1 else 0
    counts, surplus = [largest] + [least] * (amount - 1), total - largest - least * (amount - 1)
    while surplus > 0:
        movable = [i for i in range(1, amount) if counts[i] < largest] or [i for i in range(1, amount) if counts[i] < reach]
        pool, budget = sum([portions[i] for i in movable]), surplus
        for i in movable:
            more = min(reach - counts[i], max(1, budget * portions[i] // pool), surplus)
            counts[i] = counts[i] + more
            surplus = surplus - more
    return np.array(counts)


def noise(key, shape, deviation, most, shards=(), kind=jnp.bfloat16):
    array = deviation * jax.random.normal(key, shape, jnp.float32)
    if shards:
        array = array * level_of(key, shape, shards, -0.22, 0.18)
    return jnp.clip(array, -most, most).astype(kind)


def gaussian_with(key, extent, deviation, most, pieces, heavy, kind=jnp.bfloat16):
    entries = deviation * jax.random.normal(key, extent, jnp.float32)
    if pieces:
        entries = entries * level_of(key, extent, pieces, -0.22, 0.18)
    return jnp.clip(spiked(entries, jax.random.fold_in(key, 3), *heavy), -most, most).astype(kind)


def setup_inputs(seed: int = 0) -> dict:
    arg_keys = jax.random.split(jax.random.key(seed), 14)
    queries = draw_queries(jax.random.fold_in(arg_keys[13], 71), 0)
    new_key = draw_new_key(jax.random.fold_in(arg_keys[13], 71), 0)
    new_value = noise(arg_keys[2], (ROWS, HEADS * HD), 1.0, 6.0, ((0, 8), (1, 16)))
    key_cache = draw_key_cache(jax.random.fold_in(arg_keys[13], 71), 0)
    value_cache = noise(arg_keys[4], (ROWS, HEADS, CACHE_LEN, HD), 1.0, 6.0, ((0, 8), (1, 16)))
    cache_lengths = draw_cache_lengths(jax.random.fold_in(arg_keys[13], 71), 0)
    residual = noise(arg_keys[6], (ROWS, D), 0.25, 1.5, ((0, 8),))
    out_weight = gaussian_with(arg_keys[7], (HEADS * HD, D), (HEADS * HD) ** -0.5, 0.125, ((0, 16),), (0, 1, 16, 2.0))
    norm_gain = jnp.clip(1.0 + 0.15 * jax.random.normal(arg_keys[8], (D,), jnp.float32), 0.25, 1.75).astype(jnp.bfloat16)
    expert_ids_keys = jax.random.split(jax.random.fold_in(arg_keys[9], 1), ROWS // REQ_DEV)
    expert_ids_turns = jax.random.permutation(jax.random.fold_in(arg_keys[9], 3), ROWS // REQ_DEV)
    expert_ids = jax.vmap(lambda own, number: routed_block(jax.random.fold_in(arg_keys[9], 2), own, number, REQ_DEV, EXPERTS, 2, CAP, 2))(expert_ids_keys, expert_ids_turns).reshape((ROWS, 2))
    gate_weight = noise(arg_keys[10], (EXPERTS, D, FF), D ** -0.5, 0.09375, ((0, 8), (2, 16)))
    up_weight = noise(arg_keys[11], (EXPERTS, D, FF), D ** -0.5, 0.09375, ((0, 8), (2, 16)))
    down_weight = gaussian_with(arg_keys[12], (EXPERTS, FF, D), FF ** -0.5, 0.078125, ((0, 8), (1, 16)), (1, 2, 16, 2.0))
    return dict(queries=queries, new_key=new_key, new_value=new_value, key_cache=key_cache, value_cache=value_cache, cache_lengths=cache_lengths, residual=residual, out_weight=out_weight, norm_gain=norm_gain, expert_ids=expert_ids, gate_weight=gate_weight, up_weight=up_weight, down_weight=down_weight)


epsilon = 1e-05

def attend_block(block):
    query_rows, own_key, own_value, keys, values, lengths = block
    count = query_rows.shape[0]
    scale = 1.0 / math.sqrt(HD)
    query_heads = query_rows.reshape(count, HEADS, HD).astype(jnp.float32)
    key_heads = own_key.reshape(count, HEADS, HD).astype(jnp.float32)
    value_heads = own_value.reshape(count, HEADS, HD).astype(jnp.float32)
    scores = jnp.einsum('rhd,rhld->rhl', query_heads, keys.astype(jnp.float32)) * scale
    own_score = lax.optimization_barrier(jnp.sum(query_heads * key_heads, axis=-1)) * scale
    valid = jnp.arange(CACHE_LEN, dtype=jnp.int32)[None, None, :] < lengths[:, None, None]
    masked = jnp.where(valid, scores, jnp.float32(-1e+30))
    highest = jnp.maximum(lax.optimization_barrier(jnp.max(masked, axis=-1)), own_score)
    weights = jnp.where(valid, jnp.exp(masked - highest[..., None]), jnp.float32(0.0))
    own_weight = jnp.exp(own_score - highest)
    total = lax.optimization_barrier(jnp.sum(weights, axis=-1)) + own_weight
    rounded = lax.optimization_barrier(weights.astype(jnp.bfloat16)).astype(jnp.float32)
    own_rounded = lax.optimization_barrier(own_weight.astype(jnp.bfloat16)).astype(jnp.float32)
    mixed = jnp.einsum('rhl,rhld->rhd', rounded, values.astype(jnp.float32))
    mixed = mixed + own_rounded[..., None] * value_heads
    return (mixed / total[..., None]).reshape(count, HEADS * HD).astype(jnp.bfloat16)

def run_expert(operands):
    bucket, gate_w, up_w, down_w = operands
    gate = jnp.dot(bucket, gate_w, preferred_element_type=jnp.float32)
    up_part = jnp.dot(bucket, up_w, preferred_element_type=jnp.float32)
    inner = (jax.nn.silu(gate) * up_part).astype(jnp.bfloat16)
    return jnp.dot(inner, down_w, preferred_element_type=jnp.float32).astype(jnp.bfloat16)

def reference(queries, new_key, new_value, key_cache, value_cache, cache_lengths, residual, out_weight, norm_gain, expert_ids, gate_weight, up_weight, down_weight):
    blocks = (queries.reshape(N_EXPERT, REQ_DEV, HEADS * HD), new_key.reshape(N_EXPERT, REQ_DEV, HEADS * HD), new_value.reshape(N_EXPERT, REQ_DEV, HEADS * HD), key_cache.reshape(N_EXPERT, REQ_DEV, HEADS, CACHE_LEN, HD), value_cache.reshape(N_EXPERT, REQ_DEV, HEADS, CACHE_LEN, HD), cache_lengths.reshape(N_EXPERT, REQ_DEV))
    attended = lax.map(attend_block, blocks).reshape(ROWS, HEADS * HD)
    projected = jnp.dot(attended, out_weight, preferred_element_type=jnp.float32)
    stream = (residual.astype(jnp.float32) + projected).astype(jnp.bfloat16)
    stream_wide = stream.astype(jnp.float32)
    mean_square = lax.optimization_barrier(jnp.mean(stream_wide * stream_wide, axis=1, keepdims=True))
    normed = (stream_wide * lax.rsqrt(mean_square + epsilon) * norm_gain.astype(jnp.float32)).astype(jnp.bfloat16)
    onehot = (expert_ids[:, :, None] == jnp.arange(EXPERTS, dtype=jnp.int32)[None, None, :]).astype(jnp.int32)
    blocked = onehot.reshape(N_EXPERT, REQ_DEV * 2, EXPERTS)
    before = (jnp.cumsum(blocked, axis=1).astype(jnp.int32) - blocked).astype(jnp.int32)
    slots = lax.optimization_barrier(jnp.sum(before * blocked, axis=2)).astype(jnp.int32).reshape(ROWS, 2)
    block_index = (jnp.arange(ROWS, dtype=jnp.int32) // REQ_DEV).astype(jnp.int32)
    target = (expert_ids * (N_EXPERT * CAP) + block_index[:, None] * CAP + slots).astype(jnp.int32).reshape(-1)
    buckets = jnp.zeros((EXPERTS * N_EXPERT * CAP, D), jnp.bfloat16)
    buckets = buckets.at[target].set(jnp.repeat(normed, 2, axis=0))
    buckets = buckets.reshape(EXPERTS, N_EXPERT * CAP, D)
    results = lax.map(run_expert, (buckets, gate_weight, up_weight, down_weight)).reshape(EXPERTS * N_EXPERT * CAP, D)
    picked = results[target].reshape(ROWS, 2, D).astype(jnp.float32)
    return (stream_wide + 0.5 * lax.optimization_barrier(jnp.sum(picked, axis=1))).astype(jnp.bfloat16)
```

```python
import math

import jax
import jax.numpy as jnp
from jax import lax
from jax.experimental import pallas as pl
from jax.experimental.pallas import tpu as pltpu
from jax.sharding import PartitionSpec as P

epsilon = 1e-05
bf16 = jnp.bfloat16
f32 = jnp.float32
ANY = pl.BlockSpec(memory_space=pltpu.MemorySpace.HBM)
VMEM = pl.BlockSpec(memory_space=pltpu.VMEM)

EXPERTS = 8
CAP = 32
GROUP = 16


def dot(a, b, dims):
    return lax.dot_general(a, b, (dims, ((), ())), preferred_element_type=f32)


def attend_kernel(
    lens_hbm, q_hbm, nk_hbm, nv_hbm, k_hbm, v_hbm, w_hbm, ids_hbm, out_ref, table_ref,
    lens, q, nk, nv, k, v, w, ids, attended, small_sem, k_sem, v_sem, w_sem,
):
    requests, head_count, positions, size = k.shape
    groups = requests // GROUP
    parts = out_ref.shape[0]
    width = out_ref.shape[2]
    small = [
        pltpu.make_async_copy(src, dst, small_sem.at[i])
        for i, (src, dst) in enumerate(
            ((lens_hbm, lens), (q_hbm, q), (nk_hbm, nk), (nv_hbm, nv), (ids_hbm, ids))
        )
    ]
    for copy in small:
        copy.start()
    keys, values = [], []
    for g in range(groups):
        rows = pl.ds(g * GROUP, GROUP)
        keys.append(pltpu.make_async_copy(k_hbm.at[rows], k.at[rows], k_sem.at[g]))
        values.append(pltpu.make_async_copy(v_hbm.at[rows], v.at[rows], v_sem.at[g]))
        keys[g].start()
        values[g].start()
    weight = pltpu.make_async_copy(w_hbm, w, w_sem)
    weight.start()
    for copy in small:
        copy.wait()

    slots = EXPERTS * CAP
    slot = lax.broadcasted_iota(jnp.int32, (slots, requests), 0)
    expert = slot // CAP
    named = (ids[0:1, :] == expert) | (ids[1:2, :] == expert)
    earlier = (
        lax.broadcasted_iota(jnp.int32, (requests, requests), 0)
        < lax.broadcasted_iota(jnp.int32, (requests, requests), 1)
    )
    count = dot(
        jnp.where(named, 1.0, 0.0).astype(bf16),
        jnp.where(earlier, 1.0, 0.0).astype(bf16),
        ((1,), (0,)),
    )
    taken = named & (count.astype(jnp.int32) == slot - expert * CAP)
    table_ref[...] = jnp.where(taken, 1.0, 0.0).astype(bf16)

    scale = 1.0 / math.sqrt(size)
    row = lax.broadcasted_iota(jnp.int32, (requests, requests), 0)
    col = lax.broadcasted_iota(jnp.int32, (requests, requests), 1)
    length = jnp.sum(jnp.where(row == col, lens[...], 0), axis=1, keepdims=True)
    place = lax.broadcasted_iota(jnp.int32, (GROUP, GROUP * positions), 1)
    first = lax.broadcasted_iota(jnp.int32, (GROUP, GROUP * positions), 0) * positions
    for g in range(groups):
        rows = slice(g * GROUP, (g + 1) * GROUP)
        keys[g].wait()
        values[g].wait()
        valid = (place >= first) & (place < first + length[rows])
        for h in range(head_count):
            lanes = slice(h * size, (h + 1) * size)
            query = q[rows, lanes]
            own_score = (
                jnp.sum(query.astype(f32) * nk[rows, lanes].astype(f32), axis=1, keepdims=True)
                * scale
            )
            key_rows = k[rows, h].reshape(GROUP * positions, size)
            scores = dot(query, key_rows, ((1,), (1,))) * scale
            masked = jnp.where(valid, scores, f32(-1e30))
            highest = jnp.maximum(jnp.max(masked, axis=1, keepdims=True), own_score)
            weights = jnp.where(valid, jnp.exp(masked - highest), f32(0.0))
            own_weight = jnp.exp(own_score - highest)
            total = jnp.sum(weights, axis=1, keepdims=True) + own_weight
            value_rows = v[rows, h].reshape(GROUP * positions, size)
            mixed = dot(weights.astype(bf16), value_rows, ((1,), (0,)))
            own_rounded = own_weight.astype(bf16).astype(f32)
            mixed = mixed + own_rounded * nv[rows, lanes].astype(f32)
            attended[rows, lanes] = (mixed / total).astype(bf16)
    weight.wait()
    everything = attended[...]
    for n in range(parts):
        out_ref[n] = dot(everything, w[:, n * width : (n + 1) * width], ((1,), (0,))).astype(bf16)


def attend_project(queries, new_key, new_value, key_cache, value_cache, lengths, out_weight, ids, parts):
    requests, head_count, positions, size = key_cache.shape
    width = out_weight.shape[1] // parts
    groups = requests // GROUP
    return pl.pallas_call(
        attend_kernel,
        name="attend_project",
        in_specs=[ANY] * 8,
        out_specs=[VMEM, VMEM],
        out_shape=[
            jax.ShapeDtypeStruct((parts, requests, width), bf16),
            jax.ShapeDtypeStruct((EXPERTS * CAP, requests), bf16),
        ],
        scratch_shapes=[
            pltpu.VMEM((1, requests), jnp.int32),
            pltpu.VMEM(queries.shape, bf16),
            pltpu.VMEM(queries.shape, bf16),
            pltpu.VMEM(queries.shape, bf16),
            pltpu.VMEM(key_cache.shape, bf16),
            pltpu.VMEM(value_cache.shape, bf16),
            pltpu.VMEM(out_weight.shape, bf16),
            pltpu.VMEM((2, requests), jnp.int32),
            pltpu.VMEM(queries.shape, bf16),
            pltpu.SemaphoreType.DMA((5,)),
            pltpu.SemaphoreType.DMA((groups,)),
            pltpu.SemaphoreType.DMA((groups,)),
            pltpu.SemaphoreType.DMA,
        ],
        compiler_params=pltpu.CompilerParams(vmem_limit_bytes=16 << 20),
    )(lengths[None, :], queries, new_key, new_value, key_cache, value_cache, out_weight, ids.T)


def stream_kernel(parts_ref, residual_ref, table_ref, stream_ref, outgoing_ref):
    total = residual_ref[...].astype(f32)
    projected = parts_ref[0].astype(f32)
    for n in range(1, parts_ref.shape[0]):
        projected = projected + parts_ref[n].astype(f32)
    stream = (total + projected).astype(bf16)
    stream_ref[...] = stream
    outgoing_ref[...] = dot(table_ref[...], stream, ((1,), (0,))).astype(bf16)


def make_stream(parts, own_residual, table):
    requests, columns = own_residual.shape
    return pl.pallas_call(
        stream_kernel,
        name="make_stream",
        in_specs=[VMEM] * 3,
        out_specs=[VMEM, VMEM],
        out_shape=[
            jax.ShapeDtypeStruct((requests, columns), bf16),
            jax.ShapeDtypeStruct((table.shape[0], columns), bf16),
        ],
        compiler_params=pltpu.CompilerParams(vmem_limit_bytes=8 << 20),
    )(parts, own_residual, table)


def expert_kernel(
    x_ref, gain_ref, gate_hbm, up_hbm, down_hbm, out_ref,
    gate_w, up_w, down_w, normed, gate_sem, up_sem, down_sem,
):
    parts, rows, piece = x_ref.shape
    width = parts * piece
    chunks = gate_sem.shape[0]
    span = width // chunks
    gates, ups, downs = [], [], []
    for c in range(chunks):
        at = (slice(None), pl.ds(c * span, span))
        gates.append(pltpu.make_async_copy(gate_hbm.at[at], gate_w.at[at], gate_sem.at[c]))
        ups.append(pltpu.make_async_copy(up_hbm.at[at], up_w.at[at], up_sem.at[c]))
        gates[c].start()
        ups[c].start()
    for c in range(chunks):
        at = (slice(None), pl.ds(c * span, span))
        downs.append(pltpu.make_async_copy(down_hbm.at[at], down_w.at[at], down_sem.at[c]))
        downs[c].start()
    squares = jnp.zeros((rows, piece), f32)
    for n in range(parts):
        wide = x_ref[n].astype(f32)
        squares = squares + wide * wide
    mean = jnp.sum(squares, axis=1, keepdims=True) * (1.0 / width)
    factor = lax.rsqrt(mean + epsilon)
    for n in range(parts):
        lanes = slice(n * piece, (n + 1) * piece)
        gain = gain_ref[:, lanes].astype(f32)
        normed[:, lanes] = (x_ref[n].astype(f32) * factor * gain).astype(bf16)
    gate = up = None
    for c in range(chunks):
        lanes = slice(c * span, (c + 1) * span)
        gates[c].wait()
        part = dot(gate_w[:, lanes], normed[:, lanes], ((1,), (1,)))
        gate = part if gate is None else gate + part
        ups[c].wait()
        part = dot(up_w[:, lanes], normed[:, lanes], ((1,), (1,)))
        up = part if up is None else up + part
    inner = (gate / (1.0 + jnp.exp(-gate)) * up).astype(bf16)
    per = parts // chunks
    for c in range(chunks):
        downs[c].wait()
        for n in range(c * per, (c + 1) * per):
            part = dot(inner, down_w[:, n * piece : (n + 1) * piece], ((0,), (0,)))
            out_ref[n] = part.astype(bf16)


def run_expert(x, gain, gate_weight, up_weight, down_weight):
    parts, rows, piece = x.shape
    hidden, width = down_weight.shape
    chunks = 4
    return pl.pallas_call(
        expert_kernel,
        name="run_expert",
        in_specs=[VMEM, VMEM, ANY, ANY, ANY],
        out_specs=VMEM,
        out_shape=jax.ShapeDtypeStruct(x.shape, bf16),
        scratch_shapes=[
            pltpu.VMEM((hidden, width), bf16),
            pltpu.VMEM((hidden, width), bf16),
            pltpu.VMEM((hidden, width), bf16),
            pltpu.VMEM((rows, width), bf16),
            pltpu.SemaphoreType.DMA((chunks,)),
            pltpu.SemaphoreType.DMA((chunks,)),
            pltpu.SemaphoreType.DMA((chunks,)),
        ],
        compiler_params=pltpu.CompilerParams(vmem_limit_bytes=40 << 20),
    )(x, gain[None, :], gate_weight.T, up_weight.T, down_weight)


def sum_kernel(parts_ref, out_ref):
    total = parts_ref[0].astype(f32)
    for n in range(1, parts_ref.shape[0]):
        total = total + parts_ref[n].astype(f32)
    out_ref[...] = total.astype(bf16)


def sum_parts(parts):
    return pl.pallas_call(
        sum_kernel,
        name="sum_parts",
        in_specs=[VMEM],
        out_specs=VMEM,
        out_shape=jax.ShapeDtypeStruct(parts.shape[1:], bf16),
        compiler_params=pltpu.CompilerParams(vmem_limit_bytes=8 << 20),
    )(parts)


def combine_kernel(stream_ref, returned_ref, table_ref, out_ref):
    mixed = dot(table_ref[...], returned_ref[...], ((0,), (0,)))
    out_ref[...] = (stream_ref[...].astype(f32) + 0.5 * mixed).astype(bf16)


def combine(stream, returned, table):
    return pl.pallas_call(
        combine_kernel,
        name="combine",
        in_specs=[VMEM] * 3,
        out_specs=VMEM,
        out_shape=jax.ShapeDtypeStruct(stream.shape, bf16),
        compiler_params=pltpu.CompilerParams(vmem_limit_bytes=8 << 20),
    )(stream, returned, table)


def swapped(parts, axis):
    return lax.all_to_all(parts, axis, 0, 0, tiled=True)


def per_device(
    queries, new_key, new_value, key_cache, value_cache, cache_lengths, residual,
    out_weight, norm_gain, expert_ids, gate_weight, up_weight, down_weight,
):
    requests = queries.shape[0]
    hidden_count = lax.axis_size("hidden")
    columns = out_weight.shape[1] // hidden_count
    partial_value, table = attend_project(
        queries, new_key, new_value, key_cache, value_cache, cache_lengths,
        out_weight, expert_ids, hidden_count,
    )
    own_residual = lax.dynamic_slice_in_dim(
        residual, lax.axis_index("hidden") * columns, columns, 1
    )
    stream, outgoing = make_stream(swapped(partial_value, "hidden"), own_residual, table)
    incoming = swapped(outgoing.reshape(EXPERTS, CAP, columns), "expert")
    incoming = incoming.reshape(EXPERTS * CAP, columns)
    copies = jnp.broadcast_to(incoming, (hidden_count, *incoming.shape))
    gathered = swapped(copies, "hidden")
    expert_part = run_expert(gathered, norm_gain, gate_weight[0], up_weight[0], down_weight[0])
    expert_out = sum_parts(swapped(expert_part, "hidden"))
    returned = swapped(expert_out.reshape(EXPERTS, CAP, columns), "expert")
    return combine(stream, returned.reshape(EXPERTS * CAP, columns), table)


def solution(mesh):
    return jax.shard_map(
        per_device,
        mesh=mesh,
        in_specs=(
            P("expert", "hidden"),
            P("expert", "hidden"),
            P("expert", "hidden"),
            P("expert", "hidden", None, None),
            P("expert", "hidden", None, None),
            P("expert"),
            P("expert", None),
            P("hidden", None),
            P(),
            P("expert", None),
            P("expert", None, "hidden"),
            P("expert", None, "hidden"),
            P("expert", "hidden", None),
        ),
        out_specs=P("expert", "hidden"),
        check_vma=False,
    )
```

```python
import functools
import math

import jax
import jax.numpy as jnp
from jax import lax
from jax.experimental import pallas as pl
from jax.experimental.pallas import tpu as pltpu
from jax.sharding import PartitionSpec as P

epsilon = 1e-05
bf16 = jnp.bfloat16
f32 = jnp.float32
ANY = pl.BlockSpec(memory_space=pl.ANY)
VMEM = pl.BlockSpec(memory_space=pltpu.VMEM)

EXPERTS = 8
CAP = 32
GROUP = 16
STATS = 16
STEPS = (0, 1, 3, 2)


def dot(a, b, dims):
    return lax.dot_general(a, b, (dims, ((), ())), preferred_element_type=f32)


def attend_kernel(
    lens_hbm, q_hbm, nk_hbm, nv_hbm, k_hbm, v_hbm, w_hbm, ids_hbm, out_ref, table_ref,
    lens, q, nk, nv, k, v, w, ids, attended, small_sem, k_sem, v_sem, w_sem,
):
    requests, head_count, positions, size = k.shape
    groups = requests // GROUP
    parts = out_ref.shape[0]
    width = out_ref.shape[2]
    small = [
        pltpu.make_async_copy(src, dst, small_sem.at[i])
        for i, (src, dst) in enumerate(
            ((lens_hbm, lens), (q_hbm, q), (nk_hbm, nk), (nv_hbm, nv), (ids_hbm, ids))
        )
    ]
    for copy in small:
        copy.start()
    keys, values = [], []
    for g in range(groups):
        rows = pl.ds(g * GROUP, GROUP)
        keys.append(pltpu.make_async_copy(k_hbm.at[rows], k.at[rows], k_sem.at[g]))
        values.append(pltpu.make_async_copy(v_hbm.at[rows], v.at[rows], v_sem.at[g]))
        keys[g].start()
        values[g].start()
    weight = pltpu.make_async_copy(w_hbm, w, w_sem)
    weight.start()
    for copy in small:
        copy.wait()

    slots = EXPERTS * CAP
    slot = lax.broadcasted_iota(jnp.int32, (slots, requests), 0)
    expert = slot // CAP
    named = (ids[0:1, :] == expert) | (ids[1:2, :] == expert)
    earlier = (
        lax.broadcasted_iota(jnp.int32, (requests, requests), 0)
        < lax.broadcasted_iota(jnp.int32, (requests, requests), 1)
    )
    count = dot(
        jnp.where(named, 1.0, 0.0).astype(bf16),
        jnp.where(earlier, 1.0, 0.0).astype(bf16),
        ((1,), (0,)),
    )
    taken = named & (count.astype(jnp.int32) == slot - expert * CAP)
    table_ref[...] = jnp.where(taken, 1.0, 0.0).astype(bf16)

    scale = 1.0 / math.sqrt(size)
    row = lax.broadcasted_iota(jnp.int32, (requests, requests), 0)
    col = lax.broadcasted_iota(jnp.int32, (requests, requests), 1)
    length = jnp.sum(jnp.where(row == col, lens[...], 0), axis=1, keepdims=True)
    place = lax.broadcasted_iota(jnp.int32, (GROUP, GROUP * positions), 1)
    first = lax.broadcasted_iota(jnp.int32, (GROUP, GROUP * positions), 0) * positions
    for g in range(groups):
        rows = slice(g * GROUP, (g + 1) * GROUP)
        keys[g].wait()
        values[g].wait()
        valid = (place >= first) & (place < first + length[rows])
        for h in range(head_count):
            lanes = slice(h * size, (h + 1) * size)
            query = q[rows, lanes]
            own_score = (
                jnp.sum(query.astype(f32) * nk[rows, lanes].astype(f32), axis=1, keepdims=True)
                * scale
            )
            key_rows = k[rows, h].reshape(GROUP * positions, size)
            scores = dot(query, key_rows, ((1,), (1,))) * scale
            masked = jnp.where(valid, scores, f32(-1e30))
            highest = jnp.maximum(jnp.max(masked, axis=1, keepdims=True), own_score)
            weights = jnp.where(valid, jnp.exp(masked - highest), f32(0.0))
            own_weight = jnp.exp(own_score - highest)
            total = jnp.sum(weights, axis=1, keepdims=True) + own_weight
            value_rows = v[rows, h].reshape(GROUP * positions, size)
            mixed = dot(weights.astype(bf16), value_rows, ((1,), (0,)))
            own_rounded = own_weight.astype(bf16).astype(f32)
            mixed = mixed + own_rounded * nv[rows, lanes].astype(f32)
            attended[rows, lanes] = (mixed / total).astype(bf16)
    weight.wait()
    everything = attended[...]
    for n in range(parts):
        out_ref[n] = dot(everything, w[:, n * width : (n + 1) * width], ((1,), (0,))).astype(bf16)


def attend_project(queries, new_key, new_value, key_cache, value_cache, lengths, out_weight, ids, parts):
    requests, _, _, _ = key_cache.shape
    width = out_weight.shape[1] // parts
    groups = requests // GROUP
    return pl.pallas_call(
        attend_kernel,
        name="attend_project",
        in_specs=[ANY] * 8,
        out_specs=[VMEM, VMEM],
        out_shape=[
            jax.ShapeDtypeStruct((parts, requests, width), bf16),
            jax.ShapeDtypeStruct((EXPERTS * CAP, requests), bf16),
        ],
        scratch_shapes=[
            pltpu.VMEM((1, requests), jnp.int32),
            pltpu.VMEM(queries.shape, bf16),
            pltpu.VMEM(queries.shape, bf16),
            pltpu.VMEM(queries.shape, bf16),
            pltpu.VMEM(key_cache.shape, bf16),
            pltpu.VMEM(value_cache.shape, bf16),
            pltpu.VMEM(out_weight.shape, bf16),
            pltpu.VMEM((2, requests), jnp.int32),
            pltpu.VMEM(queries.shape, bf16),
            pltpu.SemaphoreType.DMA((5,)),
            pltpu.SemaphoreType.DMA((groups,)),
            pltpu.SemaphoreType.DMA((groups,)),
            pltpu.SemaphoreType.DMA,
        ],
        compiler_params=pltpu.CompilerParams(vmem_limit_bytes=65_000_000),
    )(lengths[None, :], queries, new_key, new_value, key_cache, value_cache, out_weight, ids.T)


def own_rows(ref, k, other):
    place = lax.axis_index("expert")
    expert = (place // 2 + k) % 4 * 2 + (place + other) % 2
    return ref[pl.ds(pl.multiple_of(expert * CAP, CAP), CAP), :]


def stream_kernel(parts_ref, residual_ref, table_ref, stream_ref, *block_refs):
    total = residual_ref[...].astype(f32)
    projected = parts_ref[0].astype(f32)
    for n in range(1, parts_ref.shape[0]):
        projected = projected + parts_ref[n].astype(f32)
    stream = (total + projected).astype(bf16)
    stream_ref[...] = stream
    for k, block_ref in enumerate(block_refs):
        rows = jnp.concatenate([own_rows(table_ref, k, 0), own_rows(table_ref, k, 1)], axis=0)
        block_ref[...] = dot(rows, stream, ((1,), (0,))).astype(bf16)


def make_stream(parts, own_residual, table):
    requests, columns = own_residual.shape
    return pl.pallas_call(
        stream_kernel,
        name="make_stream",
        in_specs=[VMEM] * 3,
        out_specs=[VMEM] * 5,
        out_shape=[jax.ShapeDtypeStruct((requests, columns), bf16)]
        + [jax.ShapeDtypeStruct((2 * CAP, columns), bf16)] * 4,
        compiler_params=pltpu.CompilerParams(vmem_limit_bytes=8 << 20),
    )(parts, own_residual, table)


def load_kernel(gate_hbm, up_hbm, after, gate_w, up_w, done_ref, sems):
    rows = gate_w.shape[0]
    count = sems.shape[1]
    step = rows // count // 16 * 16
    copies = []
    for i, (source, target) in enumerate(((gate_hbm, gate_w), (up_hbm, up_w))):
        for c in range(count):
            at = pl.ds(c * step, step if c < count - 1 else rows - step * (count - 1))
            copies.append(pltpu.make_async_copy(source.at[at], target.at[at], sems.at[i, c]))
    for copy in copies:
        copy.start()
    done_ref[...] = jnp.zeros(done_ref.shape, f32)
    for copy in copies:
        copy.wait()


def load_weights(gate_weight, up_weight, after):
    width, hidden = gate_weight.shape
    return pl.pallas_call(
        load_kernel,
        name="load_weights",
        in_specs=[ANY] * 3,
        out_specs=[VMEM] * 3,
        out_shape=[pltpu.VMEM((hidden, width), bf16)] * 2
        + [jax.ShapeDtypeStruct((8, 128), f32)],
        scratch_shapes=[pltpu.SemaphoreType.DMA((2, 2))],
        cost_estimate=pl.CostEstimate(
            flops=0, bytes_accessed=8 * hidden * width, transcendentals=0
        ),
        compiler_params=pltpu.CompilerParams(vmem_limit_bytes=49 << 20),
    )(gate_weight.T, up_weight.T, after)


def prepare_kernel(*refs):
    kept, passed = refs[:4], refs[4:8]
    gain_ref, _, first_ref, second_ref = refs[8:]
    piece = kept[0].shape[1]
    half = piece // 2
    x = jnp.concatenate(
        [part for k in range(4) for part in (kept[k][:CAP], passed[k][...])], axis=0
    )
    rows = x.shape[0]
    wide = x.astype(f32)
    start = pl.multiple_of(lax.axis_index("hidden") * piece, piece)
    gain = gain_ref[:, pl.ds(start, piece)].astype(f32)
    turned = wide.T
    squares = jnp.sum(turned * turned, axis=0, keepdims=True)
    high = squares.astype(bf16).astype(f32)
    low = squares - high
    line = lax.broadcasted_iota(jnp.int32, (STATS, rows), 0)
    stats = jnp.where(line == 0, high, jnp.where(line == 1, low, 0.0))
    scaled = (wide * gain).T
    first_ref[0] = scaled[:half].astype(bf16)
    second_ref[0, :half] = scaled[half:].astype(bf16)
    second_ref[0, half:] = stats.astype(bf16)


def prepare(kept, passed, gain, loaded):
    piece = kept[0].shape[1]
    half = piece // 2
    rows = EXPERTS * CAP
    return pl.pallas_call(
        prepare_kernel,
        name="prepare",
        in_specs=[VMEM] * 10,
        out_specs=[VMEM, VMEM],
        out_shape=[
            jax.ShapeDtypeStruct((1, half, rows), bf16),
            jax.ShapeDtypeStruct((1, half + STATS, rows), bf16),
        ],
        compiler_params=pltpu.CompilerParams(vmem_limit_bytes=8 << 20),
    )(*kept, *passed, gain[None, :], loaded)


def partial_products(k, first_ref, second_ref, gate_w, up_w):
    half, rows = first_ref.shape[1:]
    hidden = lax.axis_index("hidden")
    x_at, y_at = hidden // 4, hidden % 4

    def taken(weight, offset, owners):
        return jnp.concatenate(
            [
                weight[:, pl.ds(pl.multiple_of(owner * 2 * half + offset, half), half)]
                for owner in owners
            ],
            axis=1,
        )

    def owner(kx, ky):
        return (x_at + 4 - kx) % 4 * 4 + (y_at + 4 - ky) % 4

    owners = [owner(other, k) for other in STEPS]
    x = first_ref[...].reshape(4 * half, rows)
    gate = dot(taken(gate_w, 0, owners), x, ((1,), (0,)))
    up = dot(taken(up_w, 0, owners), x, ((1,), (0,)))
    owners = [owner(k, other) for other in STEPS]
    x = second_ref[:, :half, :].reshape(4 * half, rows)
    gate = gate + dot(taken(gate_w, half, owners), x, ((1,), (0,)))
    up = up + dot(taken(up_w, half, owners), x, ((1,), (0,)))
    stats = second_ref[0, half:].astype(f32)
    for j in range(1, 4):
        stats = stats + second_ref[j, half:].astype(f32)
    return gate, up, jnp.sum(stats, axis=0, keepdims=True)


def begin_kernel(first_ref, second_ref, gate_w, up_w, gate_ref, up_ref, squares_ref):
    gate_ref[...], up_ref[...], squares_ref[...] = partial_products(
        0, first_ref, second_ref, gate_w, up_w
    )


def go_on_kernel(
    k, first_ref, second_ref, gate_w, up_w, gate_in, up_in, squares_in, gate_ref, up_ref, squares_ref
):
    gate, up, squares = partial_products(k, first_ref, second_ref, gate_w, up_w)
    gate_ref[...] = gate_in[...] + gate
    up_ref[...] = up_in[...] + up
    squares_ref[...] = squares_in[...] + squares


def finish_kernel(
    k, first_ref, second_ref, gate_w, up_w, gate_in, up_in, squares_in, down_w, *out_refs
):
    first_outs, second_outs = out_refs[:4], out_refs[4:]
    _, rows, piece = first_outs[0].shape
    gate, up, squares = partial_products(k, first_ref, second_ref, gate_w, up_w)
    squares = squares + squares_in[...]
    factor = lax.rsqrt(squares * (1.0 / (16 * piece)) + epsilon)
    gate = (gate + gate_in[...]) * factor
    up = (up + up_in[...]) * factor
    inner = (gate / (1.0 + jnp.exp(-gate)) * up).astype(bf16)
    hidden = lax.axis_index("hidden")
    for kx in range(4):
        for ky in range(4):
            owner = (hidden // 4 + kx) % 4 * 4 + (hidden % 4 + ky) % 4
            weight = down_w[:, pl.ds(pl.multiple_of(owner * piece, piece), piece)]
            part = dot(inner, weight, ((0,), (0,))).astype(bf16)
            first_outs[kx][ky] = part[:rows]
            second_outs[ky][kx] = part[rows:]


def run_expert(firsts, seconds, gate_w, up_w, down_w):
    _, half, rows = firsts[0].shape
    hidden, _ = down_w.shape
    cost = pl.CostEstimate(
        flops=16 * hidden * 4 * half * rows, bytes_accessed=1 << 22, transcendentals=0
    )
    params = pltpu.CompilerParams(vmem_limit_bytes=16 << 20)
    sums = [jax.ShapeDtypeStruct((hidden, rows), f32)] * 2 + [jax.ShapeDtypeStruct((1, rows), f32)]
    state = pl.pallas_call(
        begin_kernel,
        name="expert_begin",
        in_specs=[VMEM] * 4,
        out_specs=[VMEM] * 3,
        out_shape=sums,
        cost_estimate=cost,
        compiler_params=params,
    )(firsts[0], seconds[0], gate_w, up_w)
    for i in (1, 2):
        state = pl.pallas_call(
            functools.partial(go_on_kernel, STEPS[i]),
            name="expert_go_on",
            in_specs=[VMEM] * 7,
            out_specs=[VMEM] * 3,
            out_shape=sums,
            cost_estimate=cost,
            input_output_aliases={4: 0, 5: 1, 6: 2},
            compiler_params=params,
        )(firsts[i], seconds[i], gate_w, up_w, *state)
    return pl.pallas_call(
        functools.partial(finish_kernel, STEPS[3]),
        name="expert_finish",
        in_specs=[VMEM] * 8,
        out_specs=[VMEM] * 8,
        out_shape=[jax.ShapeDtypeStruct((4, rows // 2, 2 * half), bf16)] * 8,
        cost_estimate=cost,
        compiler_params=params,
    )(firsts[3], seconds[3], gate_w, up_w, *state, down_w)


def add_kernel(*refs):
    parts, out_refs = refs[:4], refs[4:]
    for j, out_ref in enumerate(out_refs):
        total = parts[0][j].astype(f32)
        for part in parts[1:]:
            total = total + part[j].astype(f32)
        out_ref[...] = total.astype(bf16)


def add_parts(parts):
    count, rows, piece = parts[0].shape
    return list(pl.pallas_call(
        add_kernel,
        name="add_parts",
        in_specs=[VMEM] * 4,
        out_specs=[VMEM] * count,
        out_shape=[jax.ShapeDtypeStruct((rows, piece), bf16)] * count,
        compiler_params=pltpu.CompilerParams(vmem_limit_bytes=8 << 20),
    )(*parts))


def total_kernel(*refs):
    out_ref = refs[8]
    place = lax.axis_index("expert")
    for h in range(2):
        total = refs[h * 4][...].astype(f32)
        for part in refs[h * 4 + 1 : h * 4 + 4]:
            total = total + part[...].astype(f32)
        total = total.astype(bf16)
        for i in range(4):
            k, other = h * 2 + i // 2, i % 2
            block = (place // 2 + 4 - k) % 4 * 2 + (place + other) % 2
            out_ref[block] = total[i * CAP : (i + 1) * CAP]


def total_parts(firsts, seconds):
    piece = firsts[0].shape[1]
    return pl.pallas_call(
        total_kernel,
        name="total_parts",
        in_specs=[VMEM] * 8,
        out_specs=VMEM,
        out_shape=jax.ShapeDtypeStruct((EXPERTS, CAP, piece), bf16),
        compiler_params=pltpu.CompilerParams(vmem_limit_bytes=8 << 20),
    )(*firsts, *seconds)


def combine_kernel(stream_ref, returned_ref, table_ref, out_ref):
    mixed = dot(table_ref[...], returned_ref[...], ((0,), (0,)))
    out_ref[...] = (stream_ref[...].astype(f32) + 0.5 * mixed).astype(bf16)


def combine(stream, returned, table):
    return pl.pallas_call(
        combine_kernel,
        name="combine",
        in_specs=[VMEM] * 3,
        out_specs=VMEM,
        out_shape=jax.ShapeDtypeStruct(stream.shape, bf16),
        compiler_params=pltpu.CompilerParams(vmem_limit_bytes=8 << 20),
    )(stream, returned, table)


def swapped(parts, axis):
    return lax.all_to_all(parts, axis, 0, 0, tiled=True)


def along_expert(blocks):
    kept = [blocks[0]] + [None] * 3
    for k in (2, 1, 3):
        pairs = [
            (z * 2 + c, (z + k) % 4 * 2 + c) for z in range(4) for c in range(2)
        ]
        kept[k] = lax.ppermute(blocks[k], "expert", pairs)
    pairs = [(z * 2 + c, z * 2 + 1 - c) for z in range(4) for c in range(2)]
    passed = [lax.ppermute(block[CAP:], "expert", pairs) for block in kept]
    return kept, passed


def swapped(parts, axis):
    return lax.all_to_all(parts, axis, 0, 0, tiled=True)


def shifted(array, dx, dy):
    pairs = [
        (x * 4 + y, (x + dx) % 4 * 4 + (y + dy) % 4) for x in range(4) for y in range(4)
    ]
    return lax.ppermute(array, "hidden", pairs)


def per_device(
    queries, new_key, new_value, key_cache, value_cache, cache_lengths, residual,
    out_weight, norm_gain, expert_ids, gate_weight, up_weight, down_weight,
):
    hidden_count = lax.axis_size("hidden")
    columns = out_weight.shape[1] // hidden_count
    partial_value, table = attend_project(
        queries, new_key, new_value, key_cache, value_cache, cache_lengths,
        out_weight, expert_ids, hidden_count,
    )
    own_residual = lax.dynamic_slice_in_dim(
        residual, lax.axis_index("hidden") * columns, columns, 1
    )
    stream, *blocks = make_stream(swapped(partial_value, "hidden"), own_residual, table)
    gate_w, up_w, loaded = load_weights(gate_weight[0], up_weight[0], stream)
    kept, passed = along_expert(blocks)
    first, second = prepare(kept, passed, norm_gain, loaded)
    first = jnp.concatenate([first] + [shifted(first, k, 0) for k in STEPS[1:]], axis=0)
    second = jnp.concatenate([second] + [shifted(second, 0, k) for k in STEPS[1:]], axis=0)
    firsts = [first] + [shifted(first, 0, k) for k in STEPS[1:]]
    seconds = [second] + [shifted(second, k, 0) for k in STEPS[1:]]
    parts = list(run_expert(firsts, seconds, gate_w, up_w, down_weight[0]))
    firsts = add_parts(parts[:1] + [shifted(parts[k], k, 0) for k in range(1, 4)])
    seconds = add_parts(parts[4:5] + [shifted(parts[4 + k], 0, k) for k in range(1, 4)])
    firsts = firsts[:1] + [shifted(firsts[k], 0, k) for k in range(1, 4)]
    seconds = seconds[:1] + [shifted(seconds[k], k, 0) for k in range(1, 4)]
    returned = swapped(total_parts(firsts, seconds), "expert")
    return combine(stream, returned.reshape(EXPERTS * CAP, columns), table)


def solution(mesh):
    return jax.shard_map(
        per_device,
        mesh=mesh,
        in_specs=(
            P("expert", "hidden"),
            P("expert", "hidden"),
            P("expert", "hidden"),
            P("expert", "hidden", None, None),
            P("expert", "hidden", None, None),
            P("expert"),
            P("expert", None),
            P("hidden", None),
            P(),
            P("expert", None),
            P("expert", None, "hidden"),
            P("expert", None, "hidden"),
            P("expert", "hidden", None),
        ),
        out_specs=P("expert", "hidden"),
        check_vma=False,
    )
```

```python
import functools
import math

import jax
import jax.numpy as jnp
from jax import lax
from jax.experimental import pallas as pl
from jax.experimental.pallas import tpu as pltpu
from jax.sharding import PartitionSpec as P

epsilon = 1e-05
bf16 = jnp.bfloat16
f32 = jnp.float32
ANY = pl.BlockSpec(memory_space=pl.ANY)
VMEM = pl.BlockSpec(memory_space=pltpu.VMEM)

EXPERTS = 8
CAP = 32
GROUP = 16
STATS = 16
STEPS = (0, 1, 3, 2)


def dot(a, b, dims):
    return lax.dot_general(a, b, (dims, ((), ())), preferred_element_type=f32)


def hidden_at():
    hidden = lax.axis_index("hidden")
    return hidden // 4, hidden % 4


def lanes_of(n, size, offset=0, width=None):
    step = math.gcd(size, offset) if offset else size
    return pl.ds(pl.multiple_of(n * size + offset, step), width or size)


def half_lanes(c, j, k, piece):
    x_at, y_at = hidden_at()
    owner = jnp.where(c == 0, j * 4 + (y_at + k) % 4, (x_at + k) % 4 * 4 + j)
    return pl.ds(pl.multiple_of(owner * piece + c * (piece // 2), piece // 2), piece // 2)


def core_at():
    return lax.axis_index("expert") % 2


def attend_kernel(
    lens_hbm, q_hbm, nk_hbm, nv_hbm, k_hbm, v_hbm, w_hbm, residual_hbm, ids_hbm,
    attended, given, own_residual, w_half,
    lens, q, nk, nv, k, v, ids, small_sem, k_sem, v_sem, w_sem, residual_sem,
):
    requests, head_count, positions, size = k.shape
    groups = requests // GROUP
    small = [
        pltpu.make_async_copy(src, dst, small_sem.at[i])
        for i, (src, dst) in enumerate(
            ((lens_hbm, lens), (q_hbm, q), (nk_hbm, nk), (nv_hbm, nv), (ids_hbm, ids))
        )
    ]
    for copy in small:
        copy.start()
    keys, values = [], []
    for g in range(groups):
        rows = pl.ds(g * GROUP, GROUP)
        keys.append(pltpu.make_async_copy(k_hbm.at[rows], k.at[rows], k_sem.at[g]))
        values.append(pltpu.make_async_copy(v_hbm.at[rows], v.at[rows], v_sem.at[g]))
        keys[g].start()
        values[g].start()
    c = core_at()
    piece = 2 * size
    others = []
    for j in range(4):
        here = pl.ds(j * size, size)
        there = pl.ds(piece + j * size, size)
        others.append(
            pltpu.make_async_copy(
                residual_hbm.at[:, half_lanes(c, j, 0, piece)],
                own_residual.at[:, here],
                residual_sem.at[j],
            )
        )
        others.append(
            pltpu.make_async_copy(
                residual_hbm.at[:, half_lanes(1 - c, j, 0, piece)],
                given.at[pl.ds(0, requests), there],
                residual_sem.at[4 + j],
            )
        )
    for n in range(w_half.shape[1] // size):
        source = pl.ds(pl.multiple_of(n * piece + c * size, size), size)
        others.append(
            pltpu.make_async_copy(
                w_hbm.at[:, source], w_half.at[:, pl.ds(n * size, size)], w_sem.at[n]
            )
        )
    for copy in others:
        copy.start()
    for copy in small:
        copy.wait()

    scale = 1.0 / math.sqrt(size)
    row = lax.broadcasted_iota(jnp.int32, (requests, requests), 0)
    col = lax.broadcasted_iota(jnp.int32, (requests, requests), 1)
    length = jnp.sum(jnp.where(row == col, lens[...], 0), axis=1, keepdims=True)
    place = lax.broadcasted_iota(jnp.int32, (GROUP, GROUP * positions), 1)
    first = lax.broadcasted_iota(jnp.int32, (GROUP, GROUP * positions), 0) * positions
    for g in range(groups):
        rows = slice(g * GROUP, (g + 1) * GROUP)
        keys[g].wait()
        values[g].wait()
        valid = (place >= first) & (place < first + length[rows])
        for h in range(head_count):
            lanes = slice(h * size, (h + 1) * size)
            query = q[rows, lanes]
            own_score = (
                jnp.sum(query.astype(f32) * nk[rows, lanes].astype(f32), axis=1, keepdims=True)
                * scale
            )
            key_rows = k[rows, h].reshape(GROUP * positions, size)
            scores = dot(query, key_rows, ((1,), (1,))) * scale
            masked = jnp.where(valid, scores, f32(-1e30))
            highest = jnp.maximum(jnp.max(masked, axis=1, keepdims=True), own_score)
            weights = jnp.where(valid, jnp.exp(masked - highest), f32(0.0))
            own_weight = jnp.exp(own_score - highest)
            total = jnp.sum(weights, axis=1, keepdims=True) + own_weight
            value_rows = v[rows, h].reshape(GROUP * positions, size)
            mixed = dot(weights.astype(bf16), value_rows, ((1,), (0,)))
            own_rounded = own_weight.astype(bf16).astype(f32)
            mixed = mixed + own_rounded * nv[rows, lanes].astype(f32)
            attended[rows, lanes] = (mixed / total).astype(bf16)
    for copy in others:
        copy.wait()
    given[:requests, :piece] = attended[...]
    given[requests:, :] = jnp.zeros((given.shape[0] - requests, given.shape[1]), bf16)
    given[requests : requests + 2, :requests] = ids[...].astype(f32).astype(bf16)


def attend(queries, new_key, new_value, key_cache, value_cache, lengths, out_weight, residual, ids):
    requests, _, _, size = key_cache.shape
    groups = requests // GROUP
    width = out_weight.shape[1]
    return pl.pallas_call(
        attend_kernel,
        name="attend",
        in_specs=[ANY] * 9,
        out_specs=[VMEM] * 4,
        out_shape=[
            pltpu.VMEM(queries.shape, bf16),
            pltpu.VMEM((requests + STATS, queries.shape[1] + width // 8), bf16),
            pltpu.VMEM((requests, width // 8), bf16),
            pltpu.VMEM((out_weight.shape[0], width // 2), bf16),
        ],
        scratch_shapes=[
            pltpu.VMEM((1, requests), jnp.int32),
            pltpu.VMEM(queries.shape, bf16),
            pltpu.VMEM(queries.shape, bf16),
            pltpu.VMEM(queries.shape, bf16),
            pltpu.VMEM(key_cache.shape, bf16),
            pltpu.VMEM(value_cache.shape, bf16),
            pltpu.VMEM(ids.shape, jnp.int32),
            pltpu.SemaphoreType.DMA((5,)),
            pltpu.SemaphoreType.DMA((groups,)),
            pltpu.SemaphoreType.DMA((groups,)),
            pltpu.SemaphoreType.DMA((width // 2 // size,)),
            pltpu.SemaphoreType.DMA((8,)),
        ],
        compiler_params=pltpu.CompilerParams(vmem_limit_bytes=65_000_000),
    )(lengths[None, :], queries, new_key, new_value, key_cache, value_cache, out_weight, residual, ids)


def in_core_order(own, other):
    first = core_at() == 0
    return jnp.concatenate([jnp.where(first, own, other), jnp.where(first, other, own)], axis=0)


def project_kernel(attended_ref, got_ref, w_half, *out_refs):
    piece = attended_ref.shape[1]
    half = piece // 2
    c = core_at()
    x_at, y_at = hidden_at()
    rows = in_core_order(
        attended_ref[...].astype(f32), got_ref[: attended_ref.shape[0], :piece].astype(f32)
    ).astype(bf16)
    for k, out_ref in enumerate(out_refs):
        weight = jnp.concatenate(
            [
                w_half[
                    :,
                    lanes_of(
                        jnp.where(c == 0, j * 4 + (y_at + k) % 4, (x_at + k) % 4 * 4 + j), half
                    ),
                ]
                for j in range(4)
            ],
            axis=1,
        )
        out_ref[...] = dot(rows, weight, ((1,), (0,))).astype(bf16)


def project(attended, got, w_half):
    requests = attended.shape[0]
    return list(
        pl.pallas_call(
            project_kernel,
            name="project",
            in_specs=[VMEM] * 3,
            out_specs=[VMEM] * 4,
            out_shape=[pltpu.VMEM((2 * requests, w_half.shape[1] // 4), bf16)] * 4,
            compiler_params=pltpu.CompilerParams(vmem_limit_bytes=8 << 20),
        )(attended, got, w_half)
    )


def table_kernel(ids_ref, got_ref, *table_refs):
    requests = ids_ref.shape[1]
    first = core_at() == 0
    slots = EXPERTS * CAP
    slot = lax.broadcasted_iota(jnp.int32, (slots, requests), 0)
    expert = slot // CAP
    earlier = (
        lax.broadcasted_iota(jnp.int32, (requests, requests), 0)
        < lax.broadcasted_iota(jnp.int32, (requests, requests), 1)
    )
    earlier = jnp.where(earlier, 1.0, 0.0).astype(bf16)
    own = ids_ref[...]
    other = got_ref[requests : requests + 2, :requests].astype(f32).astype(jnp.int32)
    for i, table_ref in enumerate(table_refs):
        ids = jnp.where(first, own, other) if i == 0 else jnp.where(first, other, own)
        named = (ids[0:1, :] == expert) | (ids[1:2, :] == expert)
        count = dot(jnp.where(named, 1.0, 0.0).astype(bf16), earlier, ((1,), (0,)))
        taken = named & (count.astype(jnp.int32) == slot - expert * CAP)
        table_ref[...] = jnp.where(taken, 1.0, 0.0).astype(bf16)


def tables_of(ids, got):
    return pl.pallas_call(
        table_kernel,
        name="tables_of",
        in_specs=[VMEM] * 2,
        out_specs=[VMEM] * 2,
        out_shape=[pltpu.VMEM((EXPERTS * CAP, ids.shape[1]), bf16)] * 2,
        compiler_params=pltpu.CompilerParams(vmem_limit_bytes=8 << 20),
    )(ids, got)


def stream_kernel(*refs):
    parts = refs[:4]
    residual_ref, got_ref, first_table, second_table = refs[4:8]
    own_ref, given_ref = refs[8:10]
    block_refs, held = refs[10:14], refs[14]
    rows, span = parts[0].shape
    requests, half = rows // 2, span // 4
    c = core_at()
    z = lax.axis_index("expert") // 2
    x_at, y_at = hidden_at()
    projected = parts[0][...].astype(f32)
    for part in parts[1:]:
        projected = projected + part[...].astype(f32)
    residual = in_core_order(
        residual_ref[...].astype(f32), got_ref[:requests, 2 * half :].astype(f32)
    )
    held[...] = (residual + projected).astype(bf16)
    home = lanes_of(jnp.where(c == 0, x_at, y_at), half)
    own_ref[...] = held[pl.ds(pl.multiple_of(c * requests, requests), requests), home]
    given_ref[...] = held[pl.ds(pl.multiple_of((1 - c) * requests, requests), requests), home]
    for k, block_ref in enumerate(block_refs):
        for block, table in enumerate((first_table, second_table)):
            start = pl.multiple_of((z + k) % 4 * (2 * CAP), 2 * CAP)
            chosen = dot(
                table[pl.ds(start, 2 * CAP), :],
                held[block * requests : (block + 1) * requests],
                ((1,), (0,)),
            ).astype(bf16)
            for parity in range(2):
                at = parity * 2 * CAP + block * CAP
                block_ref[at : at + CAP] = chosen[parity * CAP : (parity + 1) * CAP]


def make_stream(parts, own_residual, got, tables):
    rows, span = parts[0].shape
    return pl.pallas_call(
        stream_kernel,
        name="make_stream",
        in_specs=[VMEM] * 8,
        out_specs=[VMEM] * 6,
        out_shape=[jax.ShapeDtypeStruct((rows // 2, span // 4), bf16)] * 2
        + [pltpu.VMEM((4 * CAP, span), bf16)] * 4,
        scratch_shapes=[pltpu.VMEM((rows, span), bf16)],
        compiler_params=pltpu.CompilerParams(vmem_limit_bytes=8 << 20),
    )(*parts, own_residual, got, *tables)


def plus_kernel(*refs):
    total = refs[0][...].astype(f32)
    for part in refs[1:-1]:
        total = total + part[...].astype(f32)
    refs[-1][...] = total.astype(bf16)


def plus(parts):
    return pl.pallas_call(
        plus_kernel,
        name="plus",
        in_specs=[VMEM] * len(parts),
        out_specs=VMEM,
        out_shape=jax.ShapeDtypeStruct(parts[0].shape, bf16),
        compiler_params=pltpu.CompilerParams(vmem_limit_bytes=8 << 20),
    )(*parts)


def load_kernel(source, target, sems):
    rows = target.shape[0]
    count = sems.shape[0]
    step = rows // count // 16 * 16
    copies = []
    for c in range(count):
        at = pl.ds(c * step, step if c < count - 1 else rows - step * (count - 1))
        copies.append(pltpu.make_async_copy(source.at[at], target.at[at], sems.at[c]))
    for copy in copies:
        copy.start()
    for copy in copies:
        copy.wait()


def load_weight(weight):
    return pl.pallas_call(
        load_kernel,
        name="load_weight",
        in_specs=[ANY],
        out_specs=VMEM,
        out_shape=pltpu.VMEM(weight.shape, bf16),
        scratch_shapes=[pltpu.SemaphoreType.DMA((4,))],
        cost_estimate=pl.CostEstimate(
            flops=0, bytes_accessed=4 * weight.size, transcendentals=0
        ),
        compiler_params=pltpu.CompilerParams(vmem_limit_bytes=49 << 20),
    )(weight)


def prepare_kernel(*refs):
    kept, gain_ref, out_ref = refs[:4], refs[4], refs[6]
    span = kept[0].shape[1]
    half = span // 4
    rows = EXPERTS * CAP
    c = core_at()
    ones = jnp.ones((STATS, span), bf16)
    line = lax.broadcasted_iota(jnp.int32, (STATS, rows), 0)
    gain = jnp.concatenate(
        [gain_ref[:, half_lanes(c, j, 0, 2 * half)] for j in range(4)], axis=1
    ).astype(f32)
    for i in range(2):
        start = pl.multiple_of((c + i) % 2 * (2 * CAP), 2 * CAP)
        x = jnp.concatenate([part[pl.ds(start, 2 * CAP), :] for part in kept], axis=0)
        wide = x.astype(f32)
        out_ref[i, :span] = (wide * gain).T.astype(bf16)
        squares = wide * wide
        coarse = squares.astype(bf16)
        fine = (squares - coarse.astype(f32)).astype(bf16)
        sums = dot(ones, coarse, ((1,), (1,))) + dot(ones, fine, ((1,), (1,)))
        high = sums.astype(bf16).astype(f32)
        stats = jnp.where(line == 0, high, jnp.where(line == 1, sums - high, 0.0))
        out_ref[i, span:] = stats.astype(bf16)


def prepare(kept, gain, after):
    span = kept[0].shape[1]
    return pl.pallas_call(
        prepare_kernel,
        name="prepare",
        in_specs=[VMEM] * 6,
        out_specs=VMEM,
        out_shape=pltpu.VMEM((2, span + STATS, EXPERTS * CAP), bf16),
        compiler_params=pltpu.CompilerParams(vmem_limit_bytes=8 << 20),
    )(*kept, gain[None, :], after)


def partial_products(k, own_ref, got_ref, gate_w, up_w):
    span = own_ref.shape[1] - STATS
    half = span // 4
    c = core_at()
    gate = up = None
    for x, h in ((own_ref[0, :span], c), (got_ref[:span], 1 - c)):
        lanes = [half_lanes(h, j, 4 - k, 2 * half) for j in range(4)]
        part = dot(jnp.concatenate([gate_w[:, at] for at in lanes], axis=1), x, ((1,), (0,)))
        gate = part if gate is None else gate + part
        part = dot(jnp.concatenate([up_w[:, at] for at in lanes], axis=1), x, ((1,), (0,)))
        up = part if up is None else up + part
    stats = own_ref[0, span:].astype(f32) + got_ref[span:].astype(f32)
    return gate, up, jnp.sum(stats, axis=0, keepdims=True)


def begin_kernel(first_ref, second_ref, gate_w, up_w, gate_ref, up_ref, squares_ref):
    gate_ref[...], up_ref[...], squares_ref[...] = partial_products(
        0, first_ref, second_ref, gate_w, up_w
    )


def go_on_kernel(
    k, first_ref, second_ref, gate_w, up_w, gate_in, up_in, squares_in, gate_ref, up_ref, squares_ref
):
    gate, up, squares = partial_products(k, first_ref, second_ref, gate_w, up_w)
    gate_ref[...] = gate_in[...] + gate
    up_ref[...] = up_in[...] + up
    squares_ref[...] = squares_in[...] + squares


def finish_kernel(
    k, first_ref, second_ref, gate_w, up_w, gate_in, up_in, squares_in, down_w, *out_refs
):
    first_outs, second_outs = out_refs[:4], out_refs[4:]
    _, rows, piece = first_outs[0].shape
    gate, up, squares = partial_products(k, first_ref, second_ref, gate_w, up_w)
    squares = squares + squares_in[...]
    factor = lax.rsqrt(squares * (1.0 / (16 * piece)) + epsilon)
    gate = (gate + gate_in[...]) * factor
    up = (up + up_in[...]) * factor
    inner = (gate / (1.0 + jnp.exp(-gate)) * up).astype(bf16)
    hidden = lax.axis_index("hidden")
    for kx in range(4):
        for ky in range(4):
            owner = (hidden // 4 + kx) % 4 * 4 + (hidden % 4 + ky) % 4
            weight = down_w[:, pl.ds(pl.multiple_of(owner * piece, piece), piece)]
            part = dot(inner, weight, ((0,), (0,))).astype(bf16)
            first_outs[kx][ky] = part[:rows]
            second_outs[ky][kx] = part[rows:]


def run_expert(firsts, seconds, gate_w, up_w, down_w):
    _, lines, rows = firsts[0].shape
    half = (lines - STATS) // 4
    hidden, _ = down_w.shape
    cost = pl.CostEstimate(
        flops=16 * hidden * 4 * half * rows, bytes_accessed=1 << 22, transcendentals=0
    )
    params = pltpu.CompilerParams(vmem_limit_bytes=16 << 20)
    sums = [jax.ShapeDtypeStruct((hidden, rows), f32)] * 2 + [jax.ShapeDtypeStruct((1, rows), f32)]
    state = pl.pallas_call(
        begin_kernel,
        name="expert_begin",
        in_specs=[VMEM] * 4,
        out_specs=[VMEM] * 3,
        out_shape=sums,
        cost_estimate=cost,
        compiler_params=params,
    )(firsts[0], seconds[0], gate_w, up_w)
    for i in (1, 2):
        state = pl.pallas_call(
            functools.partial(go_on_kernel, STEPS[i]),
            name="expert_go_on",
            in_specs=[VMEM] * 7,
            out_specs=[VMEM] * 3,
            out_shape=sums,
            cost_estimate=cost,
            input_output_aliases={4: 0, 5: 1, 6: 2},
            compiler_params=params,
        )(firsts[i], seconds[i], gate_w, up_w, *state)
    return pl.pallas_call(
        functools.partial(finish_kernel, STEPS[3]),
        name="expert_finish",
        in_specs=[VMEM] * 8,
        out_specs=[VMEM] * 8,
        out_shape=[jax.ShapeDtypeStruct((4, rows // 2, 2 * half), bf16)] * 8,
        cost_estimate=cost,
        compiler_params=params,
    )(firsts[3], seconds[3], gate_w, up_w, *state, down_w)


def add_kernel(*refs):
    parts, out_refs = refs[:4], refs[4:]
    for j, out_ref in enumerate(out_refs):
        total = parts[0][j].astype(f32)
        for part in parts[1:]:
            total = total + part[j].astype(f32)
        out_ref[...] = total.astype(bf16)


def add_parts(parts):
    count, rows, piece = parts[0].shape
    return list(pl.pallas_call(
        add_kernel,
        name="add_parts",
        in_specs=[VMEM] * 4,
        out_specs=[VMEM] * count,
        out_shape=[jax.ShapeDtypeStruct((rows, piece), bf16)] * count,
        compiler_params=pltpu.CompilerParams(vmem_limit_bytes=8 << 20),
    )(*parts))


def total_kernel(*refs):
    out_ref = refs[8]
    place = lax.axis_index("expert")
    for h in range(2):
        total = refs[h * 4][...].astype(f32)
        for part in refs[h * 4 + 1 : h * 4 + 4]:
            total = total + part[...].astype(f32)
        total = total.astype(bf16)
        for i in range(4):
            block = (place // 2 + 4 - (h * 2 + i // 2)) % 4 * 2 + i % 2
            out_ref[block] = total[i * CAP : (i + 1) * CAP]


def total_parts(firsts, seconds):
    piece = firsts[0].shape[1]
    return pl.pallas_call(
        total_kernel,
        name="total_parts",
        in_specs=[VMEM] * 8,
        out_specs=VMEM,
        out_shape=jax.ShapeDtypeStruct((EXPERTS, CAP, piece), bf16),
        compiler_params=pltpu.CompilerParams(vmem_limit_bytes=8 << 20),
    )(*firsts, *seconds)


def combine_kernel(own_ref, other_ref, returned_ref, first_table, second_table, out_ref):
    first = core_at() == 0
    half = own_ref.shape[1]
    own, other = own_ref[...].astype(f32), other_ref[...].astype(f32)
    table = jnp.where(
        first, first_table[...].astype(f32), second_table[...].astype(f32)
    ).astype(bf16)
    mixed = 0.5 * dot(table, returned_ref[...], ((0,), (0,)))
    out_ref[:, :half] = (jnp.where(first, own, other) + mixed[:, :half]).astype(bf16)
    out_ref[:, half:] = (jnp.where(first, other, own) + mixed[:, half:]).astype(bf16)


def combine(own, other, returned, tables):
    return pl.pallas_call(
        combine_kernel,
        name="combine",
        in_specs=[VMEM] * 5,
        out_specs=VMEM,
        out_shape=jax.ShapeDtypeStruct((own.shape[0], returned.shape[1]), bf16),
        compiler_params=pltpu.CompilerParams(vmem_limit_bytes=8 << 20),
    )(own, other, returned, *tables)


def swapped(parts, axis):
    return lax.all_to_all(parts, axis, 0, 0, tiled=True)


def along_expert(blocks):
    kept = [blocks[0]] + [None] * 3
    for k in STEPS[1:]:
        pairs = [(z * 2 + c, (z + k) % 4 * 2 + c) for z in range(4) for c in range(2)]
        kept[k] = lax.ppermute(blocks[k], "expert", pairs)
    return kept


def to_partner(array):
    pairs = [(z * 2 + c, z * 2 + 1 - c) for z in range(4) for c in range(2)]
    return lax.ppermute(array, "expert", pairs)


def split_shift(array, k, x_core):
    pairs = []
    for place in range(128):
        c, x, y = place // 16 % 2, place // 4 % 4, place % 4
        x, y = ((x + k) % 4, y) if c == x_core else (x, (y + k) % 4)
        pairs.append((place, place // 16 * 16 + x * 4 + y))
    return lax.ppermute(array, ("expert", "hidden"), pairs)


def shifted(array, dx, dy):
    pairs = [
        (x * 4 + y, (x + dx) % 4 * 4 + (y + dy) % 4) for x in range(4) for y in range(4)
    ]
    return lax.ppermute(array, "hidden", pairs)


def per_device(
    queries, new_key, new_value, key_cache, value_cache, cache_lengths, residual,
    out_weight, norm_gain, expert_ids, gate_weight, up_weight, down_weight,
):
    hidden_count = lax.axis_size("hidden")
    columns = out_weight.shape[1] // hidden_count
    ids = expert_ids.T
    attended, given, own_residual, w_half = attend(
        queries, new_key, new_value, key_cache, value_cache, cache_lengths,
        out_weight, residual, ids,
    )
    got = to_partner(given)
    tables = tables_of(ids, got)
    parts = project(attended, got, w_half)
    gate_w = load_weight(gate_weight[0].T)
    arrived = parts[:1]
    for k in STEPS[1:]:
        arrived.append(split_shift(parts[k], k, 1))
    part = plus(arrived)
    up_w = load_weight(up_weight[0].T)
    parts = [part]
    for k in STEPS[1:]:
        parts.append(split_shift(part, k, 0))
    own_stream, given, *blocks = make_stream(parts, own_residual, got, tables)
    kept = along_expert(blocks)
    other_stream = to_partner(given)
    piece = prepare(kept, norm_gain, other_stream)
    pieces = [piece] + [split_shift(piece, k, 1) for k in STEPS[1:]]
    gots = [to_partner(piece[1]) for piece in pieces]
    parts = list(run_expert(pieces, gots, gate_w, up_w, down_weight[0]))
    firsts = add_parts(parts[:1] + [shifted(parts[k], k, 0) for k in STEPS[1:]])
    seconds = add_parts(parts[4:5] + [shifted(parts[4 + k], 0, k) for k in STEPS[1:]])
    firsts = firsts[:1] + [shifted(firsts[k], 0, k) for k in STEPS[1:]]
    seconds = seconds[:1] + [shifted(seconds[k], k, 0) for k in STEPS[1:]]
    returned = swapped(total_parts(firsts, seconds), "expert")
    return combine(
        own_stream, other_stream, returned.reshape(EXPERTS * CAP, columns), tables
    )


def solution(mesh):
    return jax.shard_map(
        per_device,
        mesh=mesh,
        in_specs=(
            P("expert", "hidden"),
            P("expert", "hidden"),
            P("expert", "hidden"),
            P("expert", "hidden", None, None),
            P("expert", "hidden", None, None),
            P("expert"),
            P("expert", None),
            P("hidden", None),
            P(),
            P("expert", None),
            P("expert", None, "hidden"),
            P("expert", None, "hidden"),
            P("expert", "hidden", None),
        ),
        out_specs=P("expert", "hidden"),
        check_vma=False,
    )
```

```python
import functools
import math

import jax
import jax.numpy as jnp
from jax import lax
from jax.experimental import pallas as pl
from jax.experimental.pallas import tpu as pltpu
from jax.sharding import PartitionSpec as P

epsilon = 1e-05
bf16 = jnp.bfloat16
f32 = jnp.float32
ANY = pl.BlockSpec(memory_space=pl.ANY)
VMEM = pl.BlockSpec(memory_space=pltpu.VMEM)

EXPERTS = 8
CAP = 32
GROUP = 16
STATS = 16
STEPS = (0, 1, 3, 2)


def dot(a, b, dims):
    return lax.dot_general(a, b, (dims, ((), ())), preferred_element_type=f32)


def hidden_at():
    hidden = lax.axis_index("hidden")
    return hidden // 4, hidden % 4


def lanes_of(n, size, offset=0, width=None):
    step = math.gcd(size, offset) if offset else size
    return pl.ds(pl.multiple_of(n * size + offset, step), width or size)


def half_lanes(c, j, k, piece):
    x_at, y_at = hidden_at()
    owner = jnp.where(c == 0, j * 4 + (y_at + k) % 4, (x_at + k) % 4 * 4 + j)
    return pl.ds(pl.multiple_of(owner * piece + c * (piece // 2), piece // 2), piece // 2)


def core_at():
    return lax.axis_index("expert") % 2


def attend_kernel(
    lens_hbm, q_hbm, nk_hbm, nv_hbm, k_hbm, v_hbm, w_hbm, residual_hbm, ids_hbm,
    attended, given, own_residual, w_half,
    lens, q, nk, nv, k, v, ids, small_sem, k_sem, v_sem, w_sem, residual_sem,
):
    requests, head_count, positions, size = k.shape
    groups = requests // GROUP
    small = [
        pltpu.make_async_copy(src, dst, small_sem.at[i])
        for i, (src, dst) in enumerate(
            ((lens_hbm, lens), (q_hbm, q), (nk_hbm, nk), (nv_hbm, nv), (ids_hbm, ids))
        )
    ]
    for copy in small:
        copy.start()
    keys, values = [], []
    for g in range(groups):
        rows = pl.ds(g * GROUP, GROUP)
        keys.append(pltpu.make_async_copy(k_hbm.at[rows], k.at[rows], k_sem.at[g]))
        values.append(pltpu.make_async_copy(v_hbm.at[rows], v.at[rows], v_sem.at[g]))
        keys[g].start()
        values[g].start()
    c = core_at()
    piece = 2 * size
    others = []
    for j in range(4):
        here = pl.ds(j * size, size)
        there = pl.ds(piece + j * size, size)
        others.append(
            pltpu.make_async_copy(
                residual_hbm.at[:, half_lanes(c, j, 0, piece)],
                own_residual.at[:, here],
                residual_sem.at[j],
            )
        )
        others.append(
            pltpu.make_async_copy(
                residual_hbm.at[:, half_lanes(1 - c, j, 0, piece)],
                given.at[pl.ds(0, requests), there],
                residual_sem.at[4 + j],
            )
        )
    for n in range(w_half.shape[1] // size):
        source = pl.ds(pl.multiple_of(n * piece + c * size, size), size)
        others.append(
            pltpu.make_async_copy(
                w_hbm.at[:, source], w_half.at[:, pl.ds(n * size, size)], w_sem.at[n]
            )
        )
    for copy in others:
        copy.start()
    for copy in small:
        copy.wait()

    scale = 1.0 / math.sqrt(size)
    row = lax.broadcasted_iota(jnp.int32, (requests, requests), 0)
    col = lax.broadcasted_iota(jnp.int32, (requests, requests), 1)
    length = jnp.sum(jnp.where(row == col, lens[...], 0), axis=1, keepdims=True)
    place = lax.broadcasted_iota(jnp.int32, (GROUP, GROUP * positions), 1)
    first = lax.broadcasted_iota(jnp.int32, (GROUP, GROUP * positions), 0) * positions
    for g in range(groups):
        rows = slice(g * GROUP, (g + 1) * GROUP)
        keys[g].wait()
        values[g].wait()
        valid = (place >= first) & (place < first + length[rows])
        for h in range(head_count):
            lanes = slice(h * size, (h + 1) * size)
            query = q[rows, lanes]
            own_score = (
                jnp.sum(query.astype(f32) * nk[rows, lanes].astype(f32), axis=1, keepdims=True)
                * scale
            )
            key_rows = k[rows, h].reshape(GROUP * positions, size)
            scores = dot(query, key_rows, ((1,), (1,))) * scale
            masked = jnp.where(valid, scores, f32(-1e30))
            highest = jnp.maximum(jnp.max(masked, axis=1, keepdims=True), own_score)
            weights = jnp.where(valid, jnp.exp(masked - highest), f32(0.0))
            own_weight = jnp.exp(own_score - highest)
            total = jnp.sum(weights, axis=1, keepdims=True) + own_weight
            value_rows = v[rows, h].reshape(GROUP * positions, size)
            mixed = dot(weights.astype(bf16), value_rows, ((1,), (0,)))
            own_rounded = own_weight.astype(bf16).astype(f32)
            mixed = mixed + own_rounded * nv[rows, lanes].astype(f32)
            attended[rows, lanes] = (mixed / total).astype(bf16)
    for copy in others:
        copy.wait()
    given[:requests, :piece] = attended[...]
    given[requests:, :] = jnp.zeros((given.shape[0] - requests, given.shape[1]), bf16)
    given[requests : requests + 2, :requests] = ids[...].astype(f32).astype(bf16)


def attend(queries, new_key, new_value, key_cache, value_cache, lengths, out_weight, residual, ids):
    requests, _, _, size = key_cache.shape
    groups = requests // GROUP
    width = out_weight.shape[1]
    return pl.pallas_call(
        attend_kernel,
        name="attend",
        in_specs=[ANY] * 9,
        out_specs=[VMEM] * 4,
        out_shape=[
            pltpu.VMEM(queries.shape, bf16),
            pltpu.VMEM((requests + STATS, queries.shape[1] + width // 8), bf16),
            pltpu.VMEM((requests, width // 8), bf16),
            pltpu.VMEM((out_weight.shape[0], width // 2), bf16),
        ],
        scratch_shapes=[
            pltpu.VMEM((1, requests), jnp.int32),
            pltpu.VMEM(queries.shape, bf16),
            pltpu.VMEM(queries.shape, bf16),
            pltpu.VMEM(queries.shape, bf16),
            pltpu.VMEM(key_cache.shape, bf16),
            pltpu.VMEM(value_cache.shape, bf16),
            pltpu.VMEM(ids.shape, jnp.int32),
            pltpu.SemaphoreType.DMA((5,)),
            pltpu.SemaphoreType.DMA((groups,)),
            pltpu.SemaphoreType.DMA((groups,)),
            pltpu.SemaphoreType.DMA((width // 2 // size,)),
            pltpu.SemaphoreType.DMA((8,)),
        ],
        compiler_params=pltpu.CompilerParams(vmem_limit_bytes=65_000_000),
    )(lengths[None, :], queries, new_key, new_value, key_cache, value_cache, out_weight, residual, ids)


def in_core_order(own, other):
    first = core_at() == 0
    return jnp.concatenate([jnp.where(first, own, other), jnp.where(first, other, own)], axis=0)


def project_kernel(attended_ref, got_ref, w_half, *out_refs):
    piece = attended_ref.shape[1]
    half = piece // 2
    c = core_at()
    x_at, y_at = hidden_at()
    rows = in_core_order(
        attended_ref[...].astype(f32), got_ref[: attended_ref.shape[0], :piece].astype(f32)
    ).astype(bf16)
    for k, out_ref in enumerate(out_refs):
        weight = jnp.concatenate(
            [
                w_half[
                    :,
                    lanes_of(
                        jnp.where(c == 0, j * 4 + (y_at + k) % 4, (x_at + k) % 4 * 4 + j), half
                    ),
                ]
                for j in range(4)
            ],
            axis=1,
        )
        out_ref[...] = dot(rows, weight, ((1,), (0,))).astype(bf16)


def project(attended, got, w_half):
    requests = attended.shape[0]
    return list(
        pl.pallas_call(
            project_kernel,
            name="project",
            in_specs=[VMEM] * 3,
            out_specs=[VMEM] * 4,
            out_shape=[pltpu.VMEM((2 * requests, w_half.shape[1] // 4), bf16)] * 4,
            compiler_params=pltpu.CompilerParams(vmem_limit_bytes=8 << 20),
        )(attended, got, w_half)
    )


def table_kernel(ids_ref, got_ref, *table_refs):
    requests = ids_ref.shape[1]
    first = core_at() == 0
    slots = EXPERTS * CAP
    slot = lax.broadcasted_iota(jnp.int32, (slots, requests), 0)
    expert = slot // CAP
    earlier = (
        lax.broadcasted_iota(jnp.int32, (requests, requests), 0)
        < lax.broadcasted_iota(jnp.int32, (requests, requests), 1)
    )
    earlier = jnp.where(earlier, 1.0, 0.0).astype(bf16)
    own = ids_ref[...]
    other = got_ref[requests : requests + 2, :requests].astype(f32).astype(jnp.int32)
    for i, table_ref in enumerate(table_refs):
        ids = jnp.where(first, own, other) if i == 0 else jnp.where(first, other, own)
        named = (ids[0:1, :] == expert) | (ids[1:2, :] == expert)
        count = dot(jnp.where(named, 1.0, 0.0).astype(bf16), earlier, ((1,), (0,)))
        taken = named & (count.astype(jnp.int32) == slot - expert * CAP)
        table_ref[...] = jnp.where(taken, 1.0, 0.0).astype(bf16)


def tables_of(ids, got):
    return pl.pallas_call(
        table_kernel,
        name="tables_of",
        in_specs=[VMEM] * 2,
        out_specs=[VMEM] * 2,
        out_shape=[pltpu.VMEM((EXPERTS * CAP, ids.shape[1]), bf16)] * 2,
        compiler_params=pltpu.CompilerParams(vmem_limit_bytes=8 << 20),
    )(ids, got)


def stream_kernel(*refs):
    parts = refs[:4]
    residual_ref, got_ref, first_table, second_table = refs[4:8]
    own_ref, given_ref = refs[8:10]
    block_refs, held = refs[10:14], refs[14]
    rows, span = parts[0].shape
    requests, half = rows // 2, span // 4
    c = core_at()
    z = lax.axis_index("expert") // 2
    x_at, y_at = hidden_at()
    projected = parts[0][...].astype(f32)
    for part in parts[1:]:
        projected = projected + part[...].astype(f32)
    residual = in_core_order(
        residual_ref[...].astype(f32), got_ref[:requests, 2 * half :].astype(f32)
    )
    held[...] = (residual + projected).astype(bf16)
    home = lanes_of(jnp.where(c == 0, x_at, y_at), half)
    own_ref[...] = held[pl.ds(pl.multiple_of(c * requests, requests), requests), home]
    given_ref[...] = held[pl.ds(pl.multiple_of((1 - c) * requests, requests), requests), home]
    for k, block_ref in enumerate(block_refs):
        for block, table in enumerate((first_table, second_table)):
            start = pl.multiple_of((z + k) % 4 * (2 * CAP), 2 * CAP)
            chosen = dot(
                table[pl.ds(start, 2 * CAP), :],
                held[block * requests : (block + 1) * requests],
                ((1,), (0,)),
            ).astype(bf16)
            for parity in range(2):
                at = parity * 2 * CAP + block * CAP
                block_ref[at : at + CAP] = chosen[parity * CAP : (parity + 1) * CAP]


def make_stream(parts, own_residual, got, tables):
    rows, span = parts[0].shape
    return pl.pallas_call(
        stream_kernel,
        name="make_stream",
        in_specs=[VMEM] * 8,
        out_specs=[VMEM] * 6,
        out_shape=[jax.ShapeDtypeStruct((rows // 2, span // 4), bf16)] * 2
        + [pltpu.VMEM((4 * CAP, span), bf16)] * 4,
        scratch_shapes=[pltpu.VMEM((rows, span), bf16)],
        compiler_params=pltpu.CompilerParams(vmem_limit_bytes=8 << 20),
    )(*parts, own_residual, got, *tables)


def plus_kernel(*refs):
    total = refs[0][...].astype(f32)
    for part in refs[1:-1]:
        total = total + part[...].astype(f32)
    refs[-1][...] = total.astype(bf16)


def plus(parts):
    return pl.pallas_call(
        plus_kernel,
        name="plus",
        in_specs=[VMEM] * len(parts),
        out_specs=VMEM,
        out_shape=jax.ShapeDtypeStruct(parts[0].shape, bf16),
        compiler_params=pltpu.CompilerParams(vmem_limit_bytes=8 << 20),
    )(*parts)


def load_kernel(source, target, sems):
    rows = target.shape[0]
    count = sems.shape[0]
    step = rows // count // 16 * 16
    copies = []
    for c in range(count):
        at = pl.ds(c * step, step if c < count - 1 else rows - step * (count - 1))
        copies.append(pltpu.make_async_copy(source.at[at], target.at[at], sems.at[c]))
    for copy in copies:
        copy.start()
    for copy in copies:
        copy.wait()


def load_weight(weight, grant):
    return pl.pallas_call(
        load_kernel,
        name="load_weight",
        in_specs=[ANY],
        out_specs=VMEM,
        out_shape=pltpu.VMEM(weight.shape, bf16),
        scratch_shapes=[pltpu.SemaphoreType.DMA((4,))],
        cost_estimate=pl.CostEstimate(
            flops=0, bytes_accessed=4 * weight.size, transcendentals=0
        ),
        compiler_params=pltpu.CompilerParams(vmem_limit_bytes=grant << 20),
    )(weight)


def prepare_kernel(*refs):
    kept, gain_ref, out_ref = refs[:4], refs[4], refs[5]
    span = kept[0].shape[1]
    half = span // 4
    rows = EXPERTS * CAP
    c = core_at()
    ones = jnp.ones((STATS, span), bf16)
    line = lax.broadcasted_iota(jnp.int32, (STATS, rows), 0)
    gain = jnp.concatenate(
        [gain_ref[:, half_lanes(c, j, 0, 2 * half)] for j in range(4)], axis=1
    ).astype(f32)
    for i in range(2):
        start = pl.multiple_of((c + i) % 2 * (2 * CAP), 2 * CAP)
        x = jnp.concatenate([part[pl.ds(start, 2 * CAP), :] for part in kept], axis=0)
        wide = x.astype(f32)
        out_ref[i, :span] = (wide * gain).T.astype(bf16)
        squares = wide * wide
        coarse = squares.astype(bf16)
        fine = (squares - coarse.astype(f32)).astype(bf16)
        sums = dot(ones, coarse, ((1,), (1,))) + dot(ones, fine, ((1,), (1,)))
        high = sums.astype(bf16).astype(f32)
        stats = jnp.where(line == 0, high, jnp.where(line == 1, sums - high, 0.0))
        out_ref[i, span:] = stats.astype(bf16)


def prepare(kept, gain):
    span = kept[0].shape[1]
    return pl.pallas_call(
        prepare_kernel,
        name="prepare",
        in_specs=[VMEM] * 5,
        out_specs=VMEM,
        out_shape=pltpu.VMEM((2, span + STATS, EXPERTS * CAP), bf16),
        compiler_params=pltpu.CompilerParams(vmem_limit_bytes=8 << 20),
    )(*kept, gain[None, :])


def partial_products(k, own_ref, got_ref, gate_w, up_w):
    span = own_ref.shape[1] - STATS
    half = span // 4
    c = core_at()
    gate = up = None
    for x, h in ((own_ref[0, :span], c), (got_ref[:span], 1 - c)):
        lanes = [half_lanes(h, j, 4 - k, 2 * half) for j in range(4)]
        part = dot(jnp.concatenate([gate_w[:, at] for at in lanes], axis=1), x, ((1,), (0,)))
        gate = part if gate is None else gate + part
        part = dot(jnp.concatenate([up_w[:, at] for at in lanes], axis=1), x, ((1,), (0,)))
        up = part if up is None else up + part
    stats = own_ref[0, span:].astype(f32) + got_ref[span:].astype(f32)
    return gate, up, jnp.sum(stats, axis=0, keepdims=True)


def begin_kernel(first_ref, second_ref, gate_w, up_w, gate_ref, up_ref, squares_ref):
    gate_ref[...], up_ref[...], squares_ref[...] = partial_products(
        0, first_ref, second_ref, gate_w, up_w
    )


def go_on_kernel(
    k, first_ref, second_ref, gate_w, up_w, gate_in, up_in, squares_in, gate_ref, up_ref, squares_ref
):
    gate, up, squares = partial_products(k, first_ref, second_ref, gate_w, up_w)
    gate_ref[...] = gate_in[...] + gate
    up_ref[...] = up_in[...] + up
    squares_ref[...] = squares_in[...] + squares


def finish_kernel(
    k, width, own_ref, got_ref, gate_w, up_w, gate_in, up_in, squares_in, inner_ref
):
    gate, up, squares = partial_products(k, own_ref, got_ref, gate_w, up_w)
    squares = squares + squares_in[...]
    factor = lax.rsqrt(squares * (1.0 / width) + epsilon)
    gate = (gate + gate_in[...]) * factor
    up = (up + up_in[...]) * factor
    inner_ref[...] = (gate / (1.0 + jnp.exp(-gate)) * up).astype(bf16)


def down_kernel(k, inner_ref, down_w, kept_ref, given_ref):
    half = kept_ref.shape[2] // 4
    c = core_at()
    inner = inner_ref[...]
    for h, out_ref, at in ((c, kept_ref, (0,)), (1 - c, given_ref, ())):
        weight = jnp.concatenate(
            [down_w[:, half_lanes(h, j, k, 2 * half)] for j in range(4)], axis=1
        )
        out_ref[at if at else ...] = dot(inner, weight, ((0,), (0,))).astype(bf16)


def down_part(k, inner, down_w):
    hidden, rows = inner.shape
    span = down_w.shape[1] // 8
    return pl.pallas_call(
        functools.partial(down_kernel, k),
        name="down_part",
        in_specs=[VMEM] * 2,
        out_specs=[VMEM] * 2,
        out_shape=[pltpu.VMEM((2, rows, span), bf16), pltpu.VMEM((rows, span), bf16)],
        cost_estimate=pl.CostEstimate(
            flops=4 * hidden * rows * span, bytes_accessed=1 << 20, transcendentals=0
        ),
        compiler_params=pltpu.CompilerParams(vmem_limit_bytes=16 << 20),
    )(inner, down_w)


def join_kernel(kept_ref, got_ref, out_ref):
    out_ref[1] = got_ref[...]


def join(kept, got):
    return pl.pallas_call(
        join_kernel,
        name="join",
        in_specs=[ANY, VMEM],
        out_specs=VMEM,
        out_shape=pltpu.VMEM(kept.shape, bf16),
        input_output_aliases={0: 0},
        compiler_params=pltpu.CompilerParams(vmem_limit_bytes=8 << 20),
    )(kept, got)


def run_expert(firsts, seconds, gate_w, up_w, width):
    _, lines, rows = firsts[0].shape
    half = (lines - STATS) // 4
    hidden = gate_w.shape[0]
    cost = pl.CostEstimate(
        flops=16 * hidden * 4 * half * rows, bytes_accessed=1 << 22, transcendentals=0
    )
    params = pltpu.CompilerParams(vmem_limit_bytes=16 << 20)
    sums = [jax.ShapeDtypeStruct((hidden, rows), f32)] * 2 + [jax.ShapeDtypeStruct((1, rows), f32)]
    state = pl.pallas_call(
        begin_kernel,
        name="expert_begin",
        in_specs=[VMEM] * 4,
        out_specs=[VMEM] * 3,
        out_shape=sums,
        cost_estimate=cost,
        compiler_params=params,
    )(firsts[0], seconds[0], gate_w, up_w)
    for i in (1, 2):
        go_on = pl.pallas_call(
            functools.partial(go_on_kernel, STEPS[i]),
            name="expert_go_on",
            in_specs=[VMEM] * 7,
            out_specs=[VMEM] * 3,
            out_shape=sums,
            cost_estimate=cost,
            input_output_aliases={4: 0, 5: 1, 6: 2},
            compiler_params=params,
        )
        state = go_on(firsts[i], seconds[i], gate_w, up_w, *state)
    return pl.pallas_call(
        functools.partial(finish_kernel, STEPS[3], width),
        name="expert_finish",
        in_specs=[VMEM] * 7,
        out_specs=VMEM,
        out_shape=jax.ShapeDtypeStruct((hidden, rows), bf16),
        cost_estimate=cost,
        compiler_params=params,
    )(firsts[3], seconds[3], gate_w, up_w, *state)


def spread_kernel(*refs):
    parts, got_ref, out_refs = refs[:4], refs[4], refs[5:]
    half = out_refs[0].shape[2]
    c = core_at()
    x_at, y_at = hidden_at()
    for k, out_ref in enumerate(out_refs):
        lanes = lanes_of(jnp.where(c == 0, (x_at + k) % 4, (y_at + k) % 4), half)
        for i in range(2):
            total = (parts[0][0, :, lanes] if i == 0 else got_ref[:, lanes]).astype(f32)
            for part in parts[1:]:
                total = total + part[i, :, lanes].astype(f32)
            out_ref[i] = total.astype(bf16)


def spread_sum(parts, got):
    _, rows, span = parts[0].shape
    return list(
        pl.pallas_call(
            spread_kernel,
            name="spread_sum",
            in_specs=[VMEM] * 5,
            out_specs=[VMEM] * 4,
            out_shape=[jax.ShapeDtypeStruct((2, rows, span // 4), bf16)] * 4,
            compiler_params=pltpu.CompilerParams(vmem_limit_bytes=8 << 20),
        )(*parts, got)
    )


def total_kernel(*refs):
    parts, out_refs = refs[:4], refs[4:]
    c = core_at()
    for k, out_ref in enumerate(out_refs):
        rows = slice(k * 2 * CAP, (k + 1) * 2 * CAP)
        totals = []
        for parity in range(2):
            i = (c + parity) % 2
            total = parts[0][i, rows].astype(f32)
            for part in parts[1:]:
                total = total + part[i, rows].astype(f32)
            totals.append(total.astype(bf16))
        for block in range(2):
            for parity in range(2):
                at = (2 * block + parity) * CAP
                out_ref[at : at + CAP] = totals[parity][block * CAP : (block + 1) * CAP]


def total_parts(parts):
    half = parts[0].shape[2]
    return list(
        pl.pallas_call(
            total_kernel,
            name="total_parts",
            in_specs=[VMEM] * 4,
            out_specs=[VMEM] * 4,
            out_shape=[jax.ShapeDtypeStruct((4 * CAP, half), bf16)] * 4,
            compiler_params=pltpu.CompilerParams(vmem_limit_bytes=8 << 20),
        )(*parts)
    )


def combine_kernel(own_ref, other_ref, *refs):
    returned, first_table, second_table = refs[:4], refs[4], refs[5]
    out_ref, given_ref = refs[6:]
    c = core_at()
    z = lax.axis_index("expert") // 2
    mixed = []
    for block, table in enumerate((first_table, second_table)):
        rows = jnp.concatenate(
            [
                table[pl.ds(pl.multiple_of((z + k) % 4 * (2 * CAP), 2 * CAP), 2 * CAP), :]
                for k in range(4)
            ],
            axis=0,
        )
        values = jnp.concatenate(
            [part[block * 2 * CAP : (block + 1) * 2 * CAP] for part in returned], axis=0
        )
        mixed.append(0.5 * dot(rows, values, ((0,), (0,))))
    own = jnp.where(c == 0, mixed[0], mixed[1]) + own_ref[...].astype(f32)
    out_ref[...] = own.astype(bf16)
    other = jnp.where(c == 0, mixed[1], mixed[0]) + other_ref[...].astype(f32)
    given_ref[...] = other.astype(bf16)


def combine(own, other, returned, tables):
    return pl.pallas_call(
        combine_kernel,
        name="combine",
        in_specs=[VMEM] * 8,
        out_specs=[VMEM] * 2,
        out_shape=[jax.ShapeDtypeStruct(own.shape, bf16)] * 2,
        compiler_params=pltpu.CompilerParams(vmem_limit_bytes=8 << 20),
    )(own, other, *returned, *tables)


def lay_kernel(own_ref, got_ref, out_ref):
    first = core_at() == 0
    half = own_ref.shape[1]
    own, got = own_ref[...].astype(f32), got_ref[...].astype(f32)
    out_ref[:, :half] = jnp.where(first, own, got).astype(bf16)
    out_ref[:, half:] = jnp.where(first, got, own).astype(bf16)


def lay_out(own, got):
    rows, half = own.shape
    return pl.pallas_call(
        lay_kernel,
        name="lay_out",
        in_specs=[VMEM] * 2,
        out_specs=VMEM,
        out_shape=jax.ShapeDtypeStruct((rows, 2 * half), bf16),
        compiler_params=pltpu.CompilerParams(vmem_limit_bytes=8 << 20),
    )(own, got)


def along_expert(blocks, sign):
    kept = [blocks[0]] + [None] * 3
    for k in STEPS[1:]:
        pairs = [(z * 2 + c, (z + sign * k) % 4 * 2 + c) for z in range(4) for c in range(2)]
        kept[k] = lax.ppermute(blocks[k], "expert", pairs)
    return kept


def to_partner(array):
    pairs = [(z * 2 + c, z * 2 + 1 - c) for z in range(4) for c in range(2)]
    return lax.ppermute(array, "expert", pairs)


def split_shift(array, k, x_core):
    pairs = []
    for place in range(128):
        c, x, y = place // 16 % 2, place // 4 % 4, place % 4
        x, y = ((x + k) % 4, y) if c == x_core else (x, (y + k) % 4)
        pairs.append((place, place // 16 * 16 + x * 4 + y))
    return lax.ppermute(array, ("expert", "hidden"), pairs)


def per_device(
    queries, new_key, new_value, key_cache, value_cache, cache_lengths, residual,
    out_weight, norm_gain, expert_ids, gate_weight, up_weight, down_weight,
):
    ids = expert_ids.T
    attended, given, own_residual, w_half = attend(
        queries, new_key, new_value, key_cache, value_cache, cache_lengths,
        out_weight, residual, ids,
    )
    got = to_partner(given)
    tables = tables_of(ids, got)
    parts = project(attended, got, w_half)
    gate_w = load_weight(gate_weight[0].T, 49)
    arrived = parts[:1]
    for k in STEPS[1:]:
        arrived.append(split_shift(parts[k], k, 1))
    part = plus(arrived)
    up_w = load_weight(up_weight[0].T, 47)
    parts = [part]
    for k in STEPS[1:]:
        parts.append(split_shift(part, k, 0))
    own_stream, other_stream, *blocks = make_stream(parts, own_residual, got, tables)
    down_w = down_weight[0]
    kept = along_expert(blocks, 1)
    piece = prepare(kept, norm_gain)
    pieces, gots = [piece], [to_partner(piece[1])]
    for k in STEPS[1:]:
        pieces.append(split_shift(piece, k, 1))
    gots += [to_partner(piece[1]) for piece in pieces[1:]]
    inner = run_expert(pieces, gots, gate_w, up_w, down_weight[0].shape[1])
    arrived = [None]
    for k in STEPS[1:] + STEPS[:1]:
        kept, given = down_part(k, inner, down_w)
        got = to_partner(given)
        if k == 0:
            arrived[0] = kept
        else:
            kept = join(kept, got)
            arrived.append(split_shift(kept, k, 1))
    parts = spread_sum(arrived, got)
    parts = total_parts(parts[:1] + [split_shift(parts[k], k, 0) for k in STEPS[1:]])
    returned = along_expert(parts, -1)
    own, given = combine(own_stream, other_stream, returned, tables)
    return lay_out(own, to_partner(given))


def solution(mesh):
    return jax.shard_map(
        per_device,
        mesh=mesh,
        in_specs=(
            P("expert", "hidden"),
            P("expert", "hidden"),
            P("expert", "hidden"),
            P("expert", "hidden", None, None),
            P("expert", "hidden", None, None),
            P("expert"),
            P("expert", None),
            P("hidden", None),
            P(),
            P("expert", None),
            P("expert", None, "hidden"),
            P("expert", None, "hidden"),
            P("expert", "hidden", None),
        ),
        out_specs=P("expert", "hidden"),
        check_vma=False,
    )
```

```python
import functools
import math

import jax
import jax.numpy as jnp
from jax import lax
from jax.experimental import pallas as pl
from jax.experimental.pallas import tpu as pltpu
from jax.sharding import PartitionSpec as P

epsilon = 1e-05
bf16 = jnp.bfloat16
f32 = jnp.float32
ANY = pl.BlockSpec(memory_space=pl.ANY)
VMEM = pl.BlockSpec(memory_space=pltpu.VMEM)

EXPERTS = 8
CAP = 32
GROUP = 32
STATS = 16
STEPS = (0, 1, 3, 2)


def dot(a, b, dims):
    return lax.dot_general(a, b, (dims, ((), ())), preferred_element_type=f32)


def hidden_at():
    hidden = lax.axis_index("hidden")
    return hidden // 4, hidden % 4


def lanes_of(n, size, offset=0, width=None):
    step = math.gcd(size, offset) if offset else size
    return pl.ds(pl.multiple_of(n * size + offset, step), width or size)


def half_lanes(c, j, k, piece):
    x_at, y_at = hidden_at()
    owner = jnp.where(c == 0, j * 4 + (y_at + k) % 4, (x_at + k) % 4 * 4 + j)
    return pl.ds(pl.multiple_of(owner * piece + c * (piece // 2), piece // 2), piece // 2)


def core_at():
    return lax.axis_index("expert") % 2


def attend_kernel(
    lens_hbm, q_hbm, nk_hbm, nv_hbm, k_hbm, v_hbm, w_hbm, residual_hbm, ids_hbm,
    attended, given, own_residual, w_half,
    lens, q, nk, nv, k, v, ids, small_sem, k_sem, v_sem, w_sem, residual_sem,
):
    requests, head_count, positions, size = k.shape
    groups = requests // GROUP
    small = [
        pltpu.make_async_copy(src, dst, small_sem.at[i])
        for i, (src, dst) in enumerate(
            ((lens_hbm, lens), (q_hbm, q), (nk_hbm, nk), (nv_hbm, nv), (ids_hbm, ids))
        )
    ]
    for copy in small:
        copy.start()
    keys, values = [], []
    for g in range(groups):
        rows = pl.ds(g * GROUP, GROUP)
        keys.append(pltpu.make_async_copy(k_hbm.at[rows], k.at[rows], k_sem.at[g]))
        values.append(pltpu.make_async_copy(v_hbm.at[rows], v.at[rows], v_sem.at[g]))
        keys[g].start()
        values[g].start()
    c = core_at()
    piece = 2 * size
    others = []
    for j in range(4):
        here = pl.ds(j * size, size)
        there = pl.ds(piece + j * size, size)
        others.append(
            pltpu.make_async_copy(
                residual_hbm.at[:, half_lanes(c, j, 0, piece)],
                own_residual.at[:, here],
                residual_sem.at[j],
            )
        )
        others.append(
            pltpu.make_async_copy(
                residual_hbm.at[:, half_lanes(1 - c, j, 0, piece)],
                given.at[pl.ds(0, requests), there],
                residual_sem.at[4 + j],
            )
        )
    for n in range(w_half.shape[1] // size):
        source = pl.ds(pl.multiple_of(n * piece + c * size, size), size)
        others.append(
            pltpu.make_async_copy(
                w_hbm.at[:, source], w_half.at[:, pl.ds(n * size, size)], w_sem.at[n]
            )
        )
    for copy in small:
        copy.wait()

    scale = 1.0 / math.sqrt(size)
    row = lax.broadcasted_iota(jnp.int32, (requests, requests), 0)
    col = lax.broadcasted_iota(jnp.int32, (requests, requests), 1)
    length = jnp.sum(jnp.where(row == col, lens[...], 0), axis=1, keepdims=True)
    place = lax.broadcasted_iota(jnp.int32, (GROUP, GROUP * positions), 1)
    first = lax.broadcasted_iota(jnp.int32, (GROUP, GROUP * positions), 0) * positions
    for g in range(groups):
        rows = slice(g * GROUP, (g + 1) * GROUP)
        keys[g].wait()
        if g == 0:
            for copy in others:
                copy.start()
        valid = (place >= first) & (place < first + length[rows])
        for h in range(head_count):
            lanes = slice(h * size, (h + 1) * size)
            query = q[rows, lanes]
            own_score = (
                jnp.sum(query.astype(f32) * nk[rows, lanes].astype(f32), axis=1, keepdims=True)
                * scale
            )
            key_rows = k[rows, h].reshape(GROUP * positions, size)
            scores = dot(query, key_rows, ((1,), (1,))) * scale
            masked = jnp.where(valid, scores, f32(-1e30))
            highest = jnp.maximum(jnp.max(masked, axis=1, keepdims=True), own_score)
            weights = jnp.where(valid, jnp.exp(masked - highest), f32(0.0))
            own_weight = jnp.exp(own_score - highest)
            total = jnp.sum(weights, axis=1, keepdims=True) + own_weight
            if h == 0:
                values[g].wait()
            value_rows = v[rows, h].reshape(GROUP * positions, size)
            mixed = dot(weights.astype(bf16), value_rows, ((1,), (0,)))
            own_rounded = own_weight.astype(bf16).astype(f32)
            mixed = mixed + own_rounded * nv[rows, lanes].astype(f32)
            attended[rows, lanes] = (mixed / total).astype(bf16)
    for copy in others:
        copy.wait()
    given[:requests, :piece] = attended[...]
    given[requests:, :] = jnp.zeros((given.shape[0] - requests, given.shape[1]), bf16)
    given[requests : requests + 2, :requests] = ids[...].astype(f32).astype(bf16)


def attend(queries, new_key, new_value, key_cache, value_cache, lengths, out_weight, residual, ids):
    requests, _, _, size = key_cache.shape
    groups = requests // GROUP
    width = out_weight.shape[1]
    return pl.pallas_call(
        attend_kernel,
        name="attend",
        in_specs=[ANY] * 9,
        out_specs=[VMEM] * 4,
        out_shape=[
            pltpu.VMEM(queries.shape, bf16),
            pltpu.VMEM((requests + STATS, queries.shape[1] + width // 8), bf16),
            pltpu.VMEM((requests, width // 8), bf16),
            pltpu.VMEM((out_weight.shape[0], width // 2), bf16),
        ],
        scratch_shapes=[
            pltpu.VMEM((1, requests), jnp.int32),
            pltpu.VMEM(queries.shape, bf16),
            pltpu.VMEM(queries.shape, bf16),
            pltpu.VMEM(queries.shape, bf16),
            pltpu.VMEM(key_cache.shape, bf16),
            pltpu.VMEM(value_cache.shape, bf16),
            pltpu.VMEM(ids.shape, jnp.int32),
            pltpu.SemaphoreType.DMA((5,)),
            pltpu.SemaphoreType.DMA((groups,)),
            pltpu.SemaphoreType.DMA((groups,)),
            pltpu.SemaphoreType.DMA((width // 2 // size,)),
            pltpu.SemaphoreType.DMA((8,)),
        ],
        compiler_params=pltpu.CompilerParams(vmem_limit_bytes=65_000_000),
    )(lengths[None, :], queries, new_key, new_value, key_cache, value_cache, out_weight, residual, ids)


def in_core_order(own, other):
    first = core_at() == 0
    return jnp.concatenate([jnp.where(first, own, other), jnp.where(first, other, own)], axis=0)


def project_kernel(attended_ref, got_ref, w_half, *out_refs):
    piece = attended_ref.shape[1]
    half = piece // 2
    c = core_at()
    x_at, y_at = hidden_at()
    rows = in_core_order(
        attended_ref[...].astype(f32), got_ref[: attended_ref.shape[0], :piece].astype(f32)
    ).astype(bf16)
    for k, out_ref in enumerate(out_refs):
        weight = jnp.concatenate(
            [
                w_half[
                    :,
                    lanes_of(
                        jnp.where(c == 0, j * 4 + (y_at + k) % 4, (x_at + k) % 4 * 4 + j), half
                    ),
                ]
                for j in range(4)
            ],
            axis=1,
        )
        out_ref[...] = dot(rows, weight, ((1,), (0,))).astype(bf16)


def project(attended, got, w_half):
    requests = attended.shape[0]
    return list(
        pl.pallas_call(
            project_kernel,
            name="project",
            in_specs=[VMEM] * 3,
            out_specs=[VMEM] * 4,
            out_shape=[pltpu.VMEM((2 * requests, w_half.shape[1] // 4), bf16)] * 4,
            compiler_params=pltpu.CompilerParams(vmem_limit_bytes=8 << 20),
        )(attended, got, w_half)
    )


def table_kernel(ids_ref, got_ref, *table_refs):
    requests = ids_ref.shape[1]
    first = core_at() == 0
    slots = EXPERTS * CAP
    slot = lax.broadcasted_iota(jnp.int32, (slots, requests), 0)
    expert = slot // CAP
    earlier = (
        lax.broadcasted_iota(jnp.int32, (requests, requests), 0)
        < lax.broadcasted_iota(jnp.int32, (requests, requests), 1)
    )
    earlier = jnp.where(earlier, 1.0, 0.0).astype(bf16)
    own = ids_ref[...]
    other = got_ref[requests : requests + 2, :requests].astype(f32).astype(jnp.int32)
    for i, table_ref in enumerate(table_refs):
        ids = jnp.where(first, own, other) if i == 0 else jnp.where(first, other, own)
        named = (ids[0:1, :] == expert) | (ids[1:2, :] == expert)
        count = dot(jnp.where(named, 1.0, 0.0).astype(bf16), earlier, ((1,), (0,)))
        taken = named & (count.astype(jnp.int32) == slot - expert * CAP)
        table_ref[...] = jnp.where(taken, 1.0, 0.0).astype(bf16)


def tables_of(ids, got):
    return pl.pallas_call(
        table_kernel,
        name="tables_of",
        in_specs=[VMEM] * 2,
        out_specs=[VMEM] * 2,
        out_shape=[pltpu.VMEM((EXPERTS * CAP, ids.shape[1]), bf16)] * 2,
        compiler_params=pltpu.CompilerParams(vmem_limit_bytes=8 << 20),
    )(ids, got)


def stream_kernel(*refs):
    parts = refs[:4]
    residual_ref, got_ref, first_table, second_table = refs[4:8]
    own_ref, given_ref = refs[8:10]
    block_refs, held = refs[10:14], refs[14]
    rows, span = parts[0].shape
    requests, half = rows // 2, span // 4
    c = core_at()
    z = lax.axis_index("expert") // 2
    x_at, y_at = hidden_at()
    projected = parts[0][...].astype(f32)
    for part in parts[1:]:
        projected = projected + part[...].astype(f32)
    residual = in_core_order(
        residual_ref[...].astype(f32), got_ref[:requests, 2 * half :].astype(f32)
    )
    held[...] = (residual + projected).astype(bf16)
    home = lanes_of(jnp.where(c == 0, x_at, y_at), half)
    own_ref[...] = held[pl.ds(pl.multiple_of(c * requests, requests), requests), home]
    given_ref[...] = held[pl.ds(pl.multiple_of((1 - c) * requests, requests), requests), home]
    for k, block_ref in enumerate(block_refs):
        for block, table in enumerate((first_table, second_table)):
            start = pl.multiple_of((z + k) % 4 * (2 * CAP), 2 * CAP)
            chosen = dot(
                table[pl.ds(start, 2 * CAP), :],
                held[block * requests : (block + 1) * requests],
                ((1,), (0,)),
            ).astype(bf16)
            for parity in range(2):
                at = parity * 2 * CAP + block * CAP
                block_ref[at : at + CAP] = chosen[parity * CAP : (parity + 1) * CAP]


def make_stream(parts, own_residual, got, tables):
    rows, span = parts[0].shape
    return pl.pallas_call(
        stream_kernel,
        name="make_stream",
        in_specs=[VMEM] * 8,
        out_specs=[VMEM] * 6,
        out_shape=[jax.ShapeDtypeStruct((rows // 2, span // 4), bf16)] * 2
        + [pltpu.VMEM((4 * CAP, span), bf16)] * 4,
        scratch_shapes=[pltpu.VMEM((rows, span), bf16)],
        compiler_params=pltpu.CompilerParams(vmem_limit_bytes=8 << 20),
    )(*parts, own_residual, got, *tables)


def plus_kernel(*refs):
    total = refs[0][...].astype(f32)
    for part in refs[1:-1]:
        total = total + part[...].astype(f32)
    refs[-1][...] = total.astype(bf16)


def plus(parts):
    return pl.pallas_call(
        plus_kernel,
        name="plus",
        in_specs=[VMEM] * len(parts),
        out_specs=VMEM,
        out_shape=jax.ShapeDtypeStruct(parts[0].shape, bf16),
        compiler_params=pltpu.CompilerParams(vmem_limit_bytes=8 << 20),
    )(*parts)


def load_kernel(source, target, sems):
    rows = target.shape[0]
    count = sems.shape[0]
    step = rows // count // 16 * 16
    copies = []
    for c in range(count):
        at = pl.ds(c * step, step if c < count - 1 else rows - step * (count - 1))
        copies.append(pltpu.make_async_copy(source.at[at], target.at[at], sems.at[c]))
    for copy in copies:
        copy.start()
    for copy in copies:
        copy.wait()


def load_weight(weight, grant):
    return pl.pallas_call(
        load_kernel,
        name="load_weight",
        in_specs=[ANY],
        out_specs=VMEM,
        out_shape=pltpu.VMEM(weight.shape, bf16),
        scratch_shapes=[pltpu.SemaphoreType.DMA((4,))],
        cost_estimate=pl.CostEstimate(
            flops=0, bytes_accessed=4 * weight.size, transcendentals=0
        ),
        compiler_params=pltpu.CompilerParams(vmem_limit_bytes=grant << 20),
    )(weight)


def prepare_kernel(*refs):
    kept, gain_ref, out_ref = refs[:4], refs[4], refs[5]
    span = kept[0].shape[1]
    half = span // 4
    rows = EXPERTS * CAP
    c = core_at()
    ones = jnp.ones((STATS, span), bf16)
    line = lax.broadcasted_iota(jnp.int32, (STATS, rows), 0)
    gain = jnp.concatenate(
        [gain_ref[:, half_lanes(c, j, 0, 2 * half)] for j in range(4)], axis=1
    ).astype(f32)
    for i in range(2):
        start = pl.multiple_of((c + i) % 2 * (2 * CAP), 2 * CAP)
        x = jnp.concatenate([part[pl.ds(start, 2 * CAP), :] for part in kept], axis=0)
        wide = x.astype(f32)
        out_ref[i, :span] = (wide * gain).T.astype(bf16)
        squares = wide * wide
        coarse = squares.astype(bf16)
        fine = (squares - coarse.astype(f32)).astype(bf16)
        sums = dot(ones, coarse, ((1,), (1,))) + dot(ones, fine, ((1,), (1,)))
        high = sums.astype(bf16).astype(f32)
        stats = jnp.where(line == 0, high, jnp.where(line == 1, sums - high, 0.0))
        out_ref[i, span:] = stats.astype(bf16)


def prepare(kept, gain):
    span = kept[0].shape[1]
    return pl.pallas_call(
        prepare_kernel,
        name="prepare",
        in_specs=[VMEM] * 5,
        out_specs=VMEM,
        out_shape=pltpu.VMEM((2, span + STATS, EXPERTS * CAP), bf16),
        compiler_params=pltpu.CompilerParams(vmem_limit_bytes=8 << 20),
    )(*kept, gain[None, :])


def partial_products(k, own_ref, got_ref, gate_w, up_w):
    span = own_ref.shape[1] - STATS
    half = span // 4
    c = core_at()
    gate = up = None
    for x, h in ((own_ref[0, :span], c), (got_ref[:span], 1 - c)):
        lanes = [half_lanes(h, j, 4 - k, 2 * half) for j in range(4)]
        part = dot(jnp.concatenate([gate_w[:, at] for at in lanes], axis=1), x, ((1,), (0,)))
        gate = part if gate is None else gate + part
        part = dot(jnp.concatenate([up_w[:, at] for at in lanes], axis=1), x, ((1,), (0,)))
        up = part if up is None else up + part
    stats = own_ref[0, span:].astype(f32) + got_ref[span:].astype(f32)
    return gate, up, jnp.sum(stats, axis=0, keepdims=True)


def begin_kernel(first_ref, second_ref, gate_w, up_w, gate_ref, up_ref, squares_ref):
    gate_ref[...], up_ref[...], squares_ref[...] = partial_products(
        0, first_ref, second_ref, gate_w, up_w
    )


def go_on_kernel(
    k, first_ref, second_ref, gate_w, up_w, gate_in, up_in, squares_in, _, gate_ref, up_ref, squares_ref
):
    gate, up, squares = partial_products(k, first_ref, second_ref, gate_w, up_w)
    gate_ref[...] = gate_in[...] + gate
    up_ref[...] = up_in[...] + up
    squares_ref[...] = squares_in[...] + squares


def finish_kernel(
    k, width, own_ref, got_ref, gate_w, up_w, gate_in, up_in, squares_in, inner_ref
):
    gate, up, squares = partial_products(k, own_ref, got_ref, gate_w, up_w)
    squares = squares + squares_in[...]
    factor = lax.rsqrt(squares * (1.0 / width) + epsilon)
    gate = (gate + gate_in[...]) * factor
    up = (up + up_in[...]) * factor
    inner_ref[...] = (gate / (1.0 + jnp.exp(-gate)) * up).astype(bf16)


def down_kernel(k, inner_ref, down_w, kept_ref, given_ref):
    half = kept_ref.shape[2] // 4
    c = core_at()
    inner = inner_ref[...]
    for h, out_ref, at in ((c, kept_ref, (0,)), (1 - c, given_ref, ())):
        weight = jnp.concatenate(
            [down_w[:, half_lanes(h, j, k, 2 * half)] for j in range(4)], axis=1
        )
        out_ref[at if at else ...] = dot(inner, weight, ((0,), (0,))).astype(bf16)


def down_part(k, inner, down_w):
    hidden, rows = inner.shape
    span = down_w.shape[1] // 8
    return pl.pallas_call(
        functools.partial(down_kernel, k),
        name="down_part",
        in_specs=[VMEM] * 2,
        out_specs=[VMEM] * 2,
        out_shape=[pltpu.VMEM((2, rows, span), bf16), pltpu.VMEM((rows, span), bf16)],
        cost_estimate=pl.CostEstimate(
            flops=4 * hidden * rows * span, bytes_accessed=1 << 20, transcendentals=0
        ),
        compiler_params=pltpu.CompilerParams(vmem_limit_bytes=16 << 20),
    )(inner, down_w)


def join_kernel(kept_ref, got_ref, out_ref):
    out_ref[1] = got_ref[...]


def join(kept, got):
    return pl.pallas_call(
        join_kernel,
        name="join",
        in_specs=[ANY, VMEM],
        out_specs=VMEM,
        out_shape=pltpu.VMEM(kept.shape, bf16),
        input_output_aliases={0: 0},
        compiler_params=pltpu.CompilerParams(vmem_limit_bytes=8 << 20),
    )(kept, got)


def run_expert(firsts, seconds, gate_w, up_w, down_w):
    _, lines, rows = firsts[0].shape
    half = (lines - STATS) // 4
    hidden, width = gate_w.shape
    cost = pl.CostEstimate(
        flops=16 * hidden * 4 * half * rows, bytes_accessed=1 << 22, transcendentals=0
    )
    params = pltpu.CompilerParams(vmem_limit_bytes=16 << 20)
    sums = [jax.ShapeDtypeStruct((hidden, rows), f32)] * 2 + [jax.ShapeDtypeStruct((1, rows), f32)]
    state = pl.pallas_call(
        begin_kernel,
        name="expert_begin",
        in_specs=[VMEM] * 4,
        out_specs=[VMEM] * 3,
        out_shape=sums,
        cost_estimate=cost,
        compiler_params=params,
    )(firsts[0], seconds[0], gate_w, up_w)
    for i in (1, 2):
        go_on = pl.pallas_call(
            functools.partial(go_on_kernel, STEPS[i]),
            name="expert_go_on",
            in_specs=[VMEM] * 8,
            out_specs=[VMEM] * 3,
            out_shape=sums,
            cost_estimate=cost,
            input_output_aliases={4: 0, 5: 1, 6: 2},
            compiler_params=params,
        )
        state = go_on(firsts[i], seconds[i], gate_w, up_w, *state, down_w)
    return pl.pallas_call(
        functools.partial(finish_kernel, STEPS[3], width),
        name="expert_finish",
        in_specs=[VMEM] * 7,
        out_specs=VMEM,
        out_shape=jax.ShapeDtypeStruct((hidden, rows), bf16),
        cost_estimate=cost,
        compiler_params=params,
    )(firsts[3], seconds[3], gate_w, up_w, *state)


def spread_kernel(*refs):
    parts, got_ref, out_refs = refs[:4], refs[4], refs[5:]
    half = out_refs[0].shape[2]
    c = core_at()
    x_at, y_at = hidden_at()
    for k, out_ref in enumerate(out_refs):
        lanes = lanes_of(jnp.where(c == 0, (x_at + k) % 4, (y_at + k) % 4), half)
        for i in range(2):
            total = (parts[0][0, :, lanes] if i == 0 else got_ref[:, lanes]).astype(f32)
            for part in parts[1:]:
                total = total + part[i, :, lanes].astype(f32)
            out_ref[i] = total.astype(bf16)


def spread_sum(parts, got):
    _, rows, span = parts[0].shape
    return list(
        pl.pallas_call(
            spread_kernel,
            name="spread_sum",
            in_specs=[VMEM] * 5,
            out_specs=[VMEM] * 4,
            out_shape=[jax.ShapeDtypeStruct((2, rows, span // 4), bf16)] * 4,
            compiler_params=pltpu.CompilerParams(vmem_limit_bytes=8 << 20),
        )(*parts, got)
    )


def total_kernel(*refs):
    parts, out_refs = refs[:4], refs[4:]
    c = core_at()
    for k, out_ref in enumerate(out_refs):
        rows = slice(k * 2 * CAP, (k + 1) * 2 * CAP)
        totals = []
        for parity in range(2):
            i = (c + parity) % 2
            total = parts[0][i, rows].astype(f32)
            for part in parts[1:]:
                total = total + part[i, rows].astype(f32)
            totals.append(total.astype(bf16))
        for block in range(2):
            for parity in range(2):
                at = (2 * block + parity) * CAP
                out_ref[at : at + CAP] = totals[parity][block * CAP : (block + 1) * CAP]


def total_parts(parts):
    half = parts[0].shape[2]
    return list(
        pl.pallas_call(
            total_kernel,
            name="total_parts",
            in_specs=[VMEM] * 4,
            out_specs=[VMEM] * 4,
            out_shape=[jax.ShapeDtypeStruct((4 * CAP, half), bf16)] * 4,
            compiler_params=pltpu.CompilerParams(vmem_limit_bytes=8 << 20),
        )(*parts)
    )


def combine_kernel(own_ref, other_ref, *refs):
    returned, first_table, second_table = refs[:4], refs[4], refs[5]
    out_ref, given_ref = refs[6:]
    c = core_at()
    z = lax.axis_index("expert") // 2
    mixed = []
    for block, table in enumerate((first_table, second_table)):
        rows = jnp.concatenate(
            [
                table[pl.ds(pl.multiple_of((z + k) % 4 * (2 * CAP), 2 * CAP), 2 * CAP), :]
                for k in range(4)
            ],
            axis=0,
        )
        values = jnp.concatenate(
            [part[block * 2 * CAP : (block + 1) * 2 * CAP] for part in returned], axis=0
        )
        mixed.append(0.5 * dot(rows, values, ((0,), (0,))))
    own = jnp.where(c == 0, mixed[0], mixed[1]) + own_ref[...].astype(f32)
    out_ref[...] = own.astype(bf16)
    other = jnp.where(c == 0, mixed[1], mixed[0]) + other_ref[...].astype(f32)
    given_ref[...] = other.astype(bf16)


def combine(own, other, returned, tables):
    return pl.pallas_call(
        combine_kernel,
        name="combine",
        in_specs=[VMEM] * 8,
        out_specs=[VMEM] * 2,
        out_shape=[jax.ShapeDtypeStruct(own.shape, bf16)] * 2,
        compiler_params=pltpu.CompilerParams(vmem_limit_bytes=8 << 20),
    )(own, other, *returned, *tables)


def lay_kernel(own_ref, got_ref, out_ref):
    first = core_at() == 0
    half = own_ref.shape[1]
    own, got = own_ref[...].astype(f32), got_ref[...].astype(f32)
    out_ref[:, :half] = jnp.where(first, own, got).astype(bf16)
    out_ref[:, half:] = jnp.where(first, got, own).astype(bf16)


def lay_out(own, got):
    rows, half = own.shape
    return pl.pallas_call(
        lay_kernel,
        name="lay_out",
        in_specs=[VMEM] * 2,
        out_specs=VMEM,
        out_shape=jax.ShapeDtypeStruct((rows, 2 * half), bf16),
        compiler_params=pltpu.CompilerParams(vmem_limit_bytes=8 << 20),
    )(own, got)


def along_expert(blocks, sign):
    kept = [blocks[0]] + [None] * 3
    for k in STEPS[1:]:
        pairs = [(z * 2 + c, (z + sign * k) % 4 * 2 + c) for z in range(4) for c in range(2)]
        kept[k] = lax.ppermute(blocks[k], "expert", pairs)
    return kept


def to_partner(array):
    pairs = [(z * 2 + c, z * 2 + 1 - c) for z in range(4) for c in range(2)]
    return lax.ppermute(array, "expert", pairs)


def split_shift(array, k, x_core):
    pairs = []
    for place in range(128):
        c, x, y = place // 16 % 2, place // 4 % 4, place % 4
        x, y = ((x + k) % 4, y) if c == x_core else (x, (y + k) % 4)
        pairs.append((place, place // 16 * 16 + x * 4 + y))
    return lax.ppermute(array, ("expert", "hidden"), pairs)


def per_device(
    queries, new_key, new_value, key_cache, value_cache, cache_lengths, residual,
    out_weight, norm_gain, expert_ids, gate_weight, up_weight, down_weight,
):
    ids = expert_ids.T
    attended, given, own_residual, w_half = attend(
        queries, new_key, new_value, key_cache, value_cache, cache_lengths,
        out_weight, residual, ids,
    )
    got = to_partner(given)
    tables = tables_of(ids, got)
    parts = project(attended, got, w_half)
    gate_w = load_weight(gate_weight[0].T, 49)
    arrived = parts[:1]
    for k in STEPS[1:]:
        arrived.append(split_shift(parts[k], k, 1))
    part = plus(arrived)
    up_w = load_weight(up_weight[0].T, 47)
    parts = [part]
    for k in STEPS[1:]:
        parts.append(split_shift(part, k, 0))
    own_stream, other_stream, *blocks = make_stream(parts, own_residual, got, tables)
    down_w = down_weight[0]
    kept = along_expert(blocks, 1)
    piece = prepare(kept, norm_gain)
    pieces, gots = [piece], [to_partner(piece[1])]
    for k in STEPS[1:]:
        pieces.append(split_shift(piece, k, 1))
    for i in range(1, 4):
        gots.append(to_partner(pieces[i][1]))
    inner = run_expert(pieces, gots, gate_w, up_w, down_w)
    arrived = [None]
    for k in (3, 1, 2, 0):
        kept, given = down_part(k, inner, down_w)
        got = to_partner(given)
        if k == 0:
            arrived[0] = kept
        else:
            kept = join(kept, got)
            arrived.append(split_shift(kept, k, 1))
    parts = spread_sum(arrived, got)
    parts = total_parts(parts[:1] + [split_shift(parts[k], k, 0) for k in STEPS[1:]])
    returned = along_expert(parts, -1)
    own, given = combine(own_stream, other_stream, returned, tables)
    return lay_out(own, to_partner(given))


def solution(mesh):
    return jax.shard_map(
        per_device,
        mesh=mesh,
        in_specs=(
            P("expert", "hidden"),
            P("expert", "hidden"),
            P("expert", "hidden"),
            P("expert", "hidden", None, None),
            P("expert", "hidden", None, None),
            P("expert"),
            P("expert", None),
            P("hidden", None),
            P(),
            P("expert", None),
            P("expert", None, "hidden"),
            P("expert", None, "hidden"),
            P("expert", "hidden", None),
        ),
        out_specs=P("expert", "hidden"),
        check_vma=False,
    )
```
